128 devices in a mesh: dp: 16 (over z, x), obj: 8 (over y, core).
Axes of the slice: x: 4, y: 4, z: 4, core: 2. Of those that a mesh axis runs over, the one named last changes fastest.
Arguments:
- object_field: float32 [2, 4096, 4096], P(None, 'dp', 'obj'), may hold values from -6 to 6
- probe_modes: float32 [4, 2, 256, 256], replicated, may hold values from -3 to 3
- amplitude: float32 [768, 256, 256], P(('dp', 'obj')), may hold values from 0.3 to 5
- offsets: int32 [768, 2], P(('dp', 'obj')), may hold values from -128 to 3967, as said below
Outputs:
- object_out: float32 [2, 4096, 4096], P(None, 'dp', 'obj')
- probe_out: float32 [4, 2, 256, 256], replicated
The draws below stay inside these ranges and needn't reach their ends.
Inputs may be any that keep to these rules, and one draw needn't show every extreme that they name: `offsets`: the position in slot n of a device's 6 slots has its patch centre (offset plus 256 / 2 in both coordinates) inside that device's tile of 256 x 512 object pixels; on every device one position's centre is the tile's first pixel and one is its last pixel.
All inputs are finite; a program needn't handle non-finite values.
Results may differ from the reference program's by a relative error of at most 0.003.
Values may be sent and summed in bfloat16 or wider, within the bound.
A program may use at most 128 MiB of HBM per device.

```python
import math
import jax
import jax.numpy as jnp
from jax import lax

P_SIZE = 256
MODES = 4
TY = 256
TX = 512
POS_DEV = 6
ITERS = 2
OY = 4096
OX = 4096
POS = 768


def draw_offsets(key, part):
    key_rows = jax.random.fold_in(key, 11)
    key_cols = jax.random.fold_in(key, 23)
    key_turn = jax.random.fold_in(key, 37)
    slot_ids = jnp.arange(POS, dtype=jnp.int32)
    device_ids = slot_ids // POS_DEV
    across_count = OX // TX
    tile_row = device_ids // across_count
    tile_col = device_ids % across_count
    row_pick = jax.random.randint(key_rows, (POS,), 0, TY, dtype=jnp.int32)
    col_pick = jax.random.randint(key_cols, (POS,), 0, TX, dtype=jnp.int32)
    rotate_by = jax.random.randint(key_turn, (POS // POS_DEV,), 0, POS_DEV, dtype=jnp.int32)
    local_slot = (slot_ids % POS_DEV + rotate_by[device_ids]) % POS_DEV
    row_pick = jnp.where(local_slot == 0, 0, jnp.where(local_slot == 1, TY - 1, row_pick))
    col_pick = jnp.where(local_slot == 0, 0, jnp.where(local_slot == 1, TX - 1, col_pick))
    half = P_SIZE // 2
    row_first = tile_row * TY + row_pick - half
    col_first = tile_col * TX + col_pick - half
    return jnp.stack([row_first, col_first], axis=1).astype(jnp.int32)


def levels(own_key, shape, cuts, least, largest):
    loudness, own = 1.0, jax.random.fold_in(own_key, 6)
    for dim, blocks in cuts:
        draws = jnp.exp(jax.random.uniform(jax.random.fold_in(own, dim), (blocks,), jnp.float32, least / len(cuts), largest / len(cuts)))
        loudness = loudness * jnp.repeat(draws, shape[dim] // blocks).reshape([-1 if axis == dim else 1 for axis in range(len(shape))])
    return loudness


def centred(rng, extent, deviation, bound, split=(), kind=jnp.bfloat16):
    values = jax.random.normal(rng, extent, jnp.float32) * deviation
    if len(split) > 0:
        values = levels(rng, extent, split, -0.22, 0.18) * values
    return jnp.clip(values, min=-bound, max=bound).astype(kind)


def setup_inputs(seed: int = 0) -> dict:
    streams_of = jax.random.split(jax.random.key(seed), 5)
    object_field = centred(streams_of[0], (2, OY, OX), 1.0, 6.0, ((1, 16), (2, 8)), jnp.float32)
    probe_modes = centred(streams_of[1], (MODES, 2, P_SIZE, P_SIZE), 0.5, 3.0, (), jnp.float32)
    amplitude = jnp.clip(jnp.exp(math.log(5.0) - 2.8134107 * jax.random.uniform(streams_of[2], (POS, P_SIZE, P_SIZE), jnp.float32) ** levels(streams_of[2], (POS, P_SIZE, P_SIZE), ((0, 128),), -0.2, 0.2)), 0.3, 5.0)
    offsets = draw_offsets(jax.random.fold_in(streams_of[4], 71), 0)
    return {"object_field": object_field, "probe_modes": probe_modes, "amplitude": amplitude, "offsets": offsets}


EPSILON = 1e-06

def dft_tables(length):
    counter = jnp.arange(length, dtype=jnp.int32)
    phase_steps = counter[:, None] * counter[None, :] % length
    angle_grid = phase_steps.astype(jnp.float32) * (2.0 * jnp.pi / length)
    norm_factor = 1.0 / jnp.sqrt(jnp.float32(length))
    real_table = (jnp.cos(angle_grid) * norm_factor).astype(jnp.bfloat16)
    imag_table = (-jnp.sin(angle_grid) * norm_factor).astype(jnp.bfloat16)
    return (real_table, imag_table)

def propagate(patches, probe_low, amplitude_block, real_table, imag_table):
    table_re = real_table.astype(jnp.float32)
    table_im = imag_table.astype(jnp.float32)
    patch_re = patches[:, 0].astype(jnp.float32)[:, None]
    patch_im = patches[:, 1].astype(jnp.float32)[:, None]
    probe_re = probe_low[:, 0].astype(jnp.float32)[None]
    probe_im = probe_low[:, 1].astype(jnp.float32)[None]
    wave_re = (probe_re * patch_re - probe_im * patch_im).astype(jnp.bfloat16).astype(jnp.float32)
    wave_im = (probe_re * patch_im + probe_im * patch_re).astype(jnp.bfloat16).astype(jnp.float32)
    half_re = jnp.einsum('kr,bmrc->bmkc', table_re, wave_re) - jnp.einsum('kr,bmrc->bmkc', table_im, wave_im)
    half_im = jnp.einsum('kr,bmrc->bmkc', table_re, wave_im) + jnp.einsum('kr,bmrc->bmkc', table_im, wave_re)
    half_re = half_re.astype(jnp.bfloat16).astype(jnp.float32)
    half_im = half_im.astype(jnp.bfloat16).astype(jnp.float32)
    far_re = jnp.einsum('bmrc,ck->bmrk', half_re, table_re) - jnp.einsum('bmrc,ck->bmrk', half_im, table_im)
    far_im = jnp.einsum('bmrc,ck->bmrk', half_re, table_im) + jnp.einsum('bmrc,ck->bmrk', half_im, table_re)
    intensity = lax.optimization_barrier(jnp.sum(far_re * far_re + far_im * far_im, axis=1))
    ratio = amplitude_block / jnp.maximum(jnp.sqrt(intensity), 1.0) - 1.0
    diff_re = (far_re * ratio[:, None]).astype(jnp.bfloat16).astype(jnp.float32)
    diff_im = (far_im * ratio[:, None]).astype(jnp.bfloat16).astype(jnp.float32)
    back_re = jnp.einsum('kr,bmrc->bmkc', table_re, diff_re) + jnp.einsum('kr,bmrc->bmkc', table_im, diff_im)
    back_im = jnp.einsum('kr,bmrc->bmkc', table_re, diff_im) - jnp.einsum('kr,bmrc->bmkc', table_im, diff_re)
    back_re = back_re.astype(jnp.bfloat16).astype(jnp.float32)
    back_im = back_im.astype(jnp.bfloat16).astype(jnp.float32)
    chi_re = jnp.einsum('bmrc,ck->bmrk', back_re, table_re) + jnp.einsum('bmrc,ck->bmrk', back_im, table_im)
    chi_im = jnp.einsum('bmrc,ck->bmrk', back_im, table_re) - jnp.einsum('bmrc,ck->bmrk', back_re, table_im)
    object_re = lax.optimization_barrier(jnp.sum(probe_re * chi_re + probe_im * chi_im, axis=1))
    object_im = lax.optimization_barrier(jnp.sum(probe_re * chi_im - probe_im * chi_re, axis=1))
    probe_re_grad = lax.optimization_barrier(jnp.sum(patch_re * chi_re + patch_im * chi_im, axis=0))
    probe_im_grad = lax.optimization_barrier(jnp.sum(patch_re * chi_im - patch_im * chi_re, axis=0))
    return (jnp.stack([object_re, object_im], axis=1), jnp.stack([probe_re_grad, probe_im_grad], axis=1))

def reference(object_field, probe_modes, amplitude, offsets):
    half = P_SIZE // 2
    real_table, imag_table = dft_tables(P_SIZE)
    top_rows = (offsets[:, 0] + half).astype(jnp.int32)
    left_cols = (offsets[:, 1] + half).astype(jnp.int32)
    zero_index = jnp.zeros((), jnp.int32)
    current = object_field
    probe = probe_modes
    block_count = POS // POS_DEV
    for turn in range(ITERS):
        object_low = current.astype(jnp.bfloat16)
        padded = jnp.pad(object_low, ((0, 0), (half, half), (half, half)))
        probe_low = probe.astype(jnp.bfloat16)
        power = lax.optimization_barrier(jnp.sum(probe_low.astype(jnp.float32) ** 2, axis=(0, 1)))
        object_scale = 1.0 / (jnp.max(power) + EPSILON)

        def block_step(carry, block_index):
            grad_pad, probe_grad = carry
            start = (block_index * POS_DEV).astype(jnp.int32)
            rows = lax.dynamic_slice_in_dim(top_rows, start, POS_DEV)
            cols = lax.dynamic_slice_in_dim(left_cols, start, POS_DEV)
            amps = lax.dynamic_slice_in_dim(amplitude, start, POS_DEV, 0)
            patches = jax.vmap(lambda row, col: lax.dynamic_slice(padded, (zero_index, row, col), (2, P_SIZE, P_SIZE)))(rows, cols)
            object_terms, probe_terms = propagate(patches, probe_low, amps, real_table, imag_table)

            def add_one(position, grid):
                row = rows[position]
                col = cols[position]
                window = lax.dynamic_slice(grid, (zero_index, row, col), (2, P_SIZE, P_SIZE))
                return lax.dynamic_update_slice(grid, window + object_terms[position], (zero_index, row, col))
            grad_pad = lax.fori_loop(0, POS_DEV, add_one, grad_pad)
            return ((grad_pad, probe_grad + probe_terms), None)
        start_grad = jnp.zeros((2, OY + P_SIZE, OX + P_SIZE), jnp.float32)
        start_probe = jnp.zeros((MODES, 2, P_SIZE, P_SIZE), jnp.float32)
        (grad_pad, probe_grad), unused = lax.scan(block_step, (start_grad, start_probe), jnp.arange(block_count, dtype=jnp.int32))
        current = current + grad_pad[:, half:half + OY, half:half + OX] * object_scale
        probe = probe + probe_grad / POS
    return (current, probe)
```

```python
import functools

import jax
import jax.numpy as jnp
import ml_dtypes
import numpy as np
from jax import lax
from jax.experimental import pallas as pl
from jax.experimental.pallas import tpu as pltpu
from jax.sharding import Mesh
from jax.sharding import PartitionSpec as P

ITERS = 2
AXES = ("dp_0", "dp_1", "obj_0", "obj_1")
EPSILON = 1e-06
F32, BF16 = jnp.float32, jnp.bfloat16
S = 256
H = S // 2
TR, TC = 256, 512
ER, EC = TR + S, TC + S
MODES, COUNT = 4, 6
ROWS = MODES * 2 * S
HALF, BLOCK, PIECE = ROWS // 2, ROWS // 32, ROWS // 128
MIB = 1 << 20


def dft_tables():
    counter = np.arange(S)
    angle = 2.0 * np.pi * (counter[:, None] * counter[None, :] % S) / S
    re = (np.cos(angle) / 16.0).astype(np.float32).astype(ml_dtypes.bfloat16)
    im = (-np.sin(angle) / 16.0).astype(np.float32).astype(ml_dtypes.bfloat16)
    return np.block([[re, -im], [im, re]]), np.block([[re, im], [-im, re]])


def propagate_body(
    offs, ext, probe, amp, plus, minus, grad, probe_grad, ext32, patch, wave, half, far
):
    n = pl.program_id(0)

    @pl.when(n == 0)
    def _():
        grad[...] = jnp.zeros_like(grad)
        probe_grad[...] = jnp.zeros_like(probe_grad)
        ext32[...] = ext[...].astype(F32)

    row, col = offs[n, 0], offs[n, 1]
    row_base = pl.multiple_of((row // 8) * 8, 8)
    row_shift = row - row_base
    col_block = col // 128
    shift = col - col_block * 128
    rows = pl.ds(row_base, S + 8)

    def cols(i):
        return pl.ds(pl.multiple_of((col_block + i) * 128, 128), 128)

    lane = lax.broadcasted_iota(jnp.int32, (S + 8, 128), 1)
    for p in range(2):
        x = [pltpu.roll(ext32[p, rows, cols(i)], lax.rem(128 - shift, 128), 1) for i in range(3)]
        for i in range(2):
            joined = jnp.where(lane < 128 - shift, x[i], x[i + 1])
            joined = pltpu.roll(joined, lax.rem(S + 8 - row_shift, S + 8), 0)
            patch[p, :, i * 128 : (i + 1) * 128] = joined[:S]
    for m in range(MODES):
        qr, qi = probe[m, 0].astype(F32), probe[m, 1].astype(F32)
        pr, pi = patch[0], patch[1]
        wave[m, :S, :] = (qr * pr - qi * pi).astype(BF16)
        wave[m, S:, :] = (qr * pi + qi * pr).astype(BF16)
        mid = jnp.dot(plus[...], wave[m], preferred_element_type=F32).astype(BF16)
        half[m * S : (m + 1) * S, :S] = mid[:S]
        half[m * S : (m + 1) * S, S:] = mid[S:]
    far[...] = jnp.dot(half[...], minus[...], preferred_element_type=F32)
    intensity = None
    for m in range(MODES):
        fr, fi = far[m * S : (m + 1) * S, :S], far[m * S : (m + 1) * S, S:]
        term = fr * fr + fi * fi
        intensity = term if intensity is None else intensity + term
    ratio = amp[0] / jnp.maximum(jnp.sqrt(intensity), 1.0) - 1.0
    for m in range(MODES):
        wave[m, :S, :] = (far[m * S : (m + 1) * S, :S] * ratio).astype(BF16)
        wave[m, S:, :] = (far[m * S : (m + 1) * S, S:] * ratio).astype(BF16)
        mid = jnp.dot(minus[...], wave[m], preferred_element_type=F32).astype(BF16)
        half[m * S : (m + 1) * S, :S] = mid[:S]
        half[m * S : (m + 1) * S, S:] = mid[S:]
    far[...] = jnp.dot(half[...], plus[...], preferred_element_type=F32)
    gr = gi = None
    for m in range(MODES):
        cr, ci = far[m * S : (m + 1) * S, :S], far[m * S : (m + 1) * S, S:]
        qr, qi = probe[m, 0].astype(F32), probe[m, 1].astype(F32)
        a, b = qr * cr + qi * ci, qr * ci - qi * cr
        gr = a if gr is None else gr + a
        gi = b if gi is None else gi + b
        pr, pi = patch[0], patch[1]
        probe_grad[m, 0] += pr * cr + pi * ci
        probe_grad[m, 1] += pr * ci - pi * cr
    for p, value in enumerate((gr, gi)):
        value = jnp.concatenate([value, jnp.zeros((8, S), F32)], 0)
        x = [
            pltpu.roll(pltpu.roll(value[:, i * 128 : (i + 1) * 128], row_shift, 0), shift, 1)
            for i in range(2)
        ]
        zero = jnp.zeros_like(x[0])
        parts = (
            jnp.where(lane >= shift, x[0], zero),
            jnp.where(lane >= shift, x[1], x[0]),
            jnp.where(lane >= shift, zero, x[1]),
        )
        for i in range(3):
            grad[p, rows, cols(i)] += parts[i]


def propagate(offs, ext, probe_low, amplitude):
    plus, minus = dft_tables()

    def whole(*shape):
        return pl.BlockSpec(shape, lambda n, o: (0,) * len(shape))

    return pl.pallas_call(
        propagate_body,
        grid_spec=pltpu.PrefetchScalarGridSpec(
            num_scalar_prefetch=1,
            grid=(COUNT,),
            in_specs=[
                whole(2, ER, EC),
                whole(MODES, 2, S, S),
                pl.BlockSpec((1, S, S), lambda n, o: (n, 0, 0)),
                whole(2 * S, 2 * S),
                whole(2 * S, 2 * S),
            ],
            out_specs=[whole(2, ER, EC), whole(MODES, 2, S, S)],
            scratch_shapes=[
                pltpu.VMEM((2, ER, EC), F32),
                pltpu.VMEM((2, S, S), F32),
                pltpu.VMEM((MODES, 2 * S, S), BF16),
                pltpu.VMEM((MODES * S, 2 * S), BF16),
                pltpu.VMEM((MODES * S, 2 * S), F32),
            ],
        ),
        out_shape=[
            jax.ShapeDtypeStruct((2, ER, EC), F32),
            jax.ShapeDtypeStruct((MODES, 2, S, S), F32),
        ],
        compiler_params=pltpu.CompilerParams(
            dimension_semantics=("arbitrary",), vmem_limit_bytes=32 * MIB
        ),
        name="propagate",
    )(offs, ext, probe_low, amplitude, jnp.asarray(plus), jnp.asarray(minus))


NEAR = [(a, b) for a in (-1, 0, 1) for b in (-1, 0, 1) if (a, b) != (0, 0)]


class Place:
    def __init__(self):
        self.z, self.x, self.y, self.c = (lax.axis_index(name) for name in AXES)
        self.dp = self.z * 4 + self.x
        self.obj = self.y * 2 + self.c
        self.yz = self.y * 4 + self.z

    def has(self, a, b):
        found = None
        for step, place, count in ((a, self.dp, 16), (b, self.obj, 8)):
            if step:
                test = place > 0 if step < 0 else place < count - 1
                found = test if found is None else jnp.logical_and(found, test)
        return found

    def near(self, a, b):
        dp, obj = self.dp + a, self.obj + b
        return (dp // 4, dp % 4, obj // 2, obj % 2)

    def sibling(self):
        return (self.z, self.x, self.y, 1 - self.c)

    def in_plane(self, d):
        other = (self.yz + d) % 16
        return other, (other % 4, self.x, other // 4, self.c)

    def in_line(self, d):
        other = (self.x + d) % 4
        return other, (self.z, other, self.y, self.c)


def greet(me, everyone):
    barrier = pltpu.get_barrier_semaphore()
    expected = jnp.int32(0)
    for a, b in NEAR:
        there = me.has(a, b)

        @pl.when(there)
        def _():
            pl.semaphore_signal(
                barrier, inc=1, device_id=me.near(a, b), device_id_type=pl.DeviceIdType.MESH
            )

        expected = expected + there.astype(jnp.int32)
    if everyone:
        others = [me.sibling()]
        others += [me.in_plane(d)[1] for d in range(1, 16)]
        others += [me.in_line(d)[1] for d in range(1, 4)]
        for other in others:
            pl.semaphore_signal(
                barrier, inc=1, device_id=other, device_id_type=pl.DeviceIdType.MESH
            )
        expected = expected + len(others)
    pl.semaphore_wait(barrier, expected)


def remote(src, dst, sems, index, device):
    return pltpu.make_async_remote_copy(
        src_ref=src,
        dst_ref=dst,
        send_sem=sems.at[0, index],
        recv_sem=sems.at[1, index],
        device_id=device,
        device_id_type=pl.DeviceIdType.MESH,
    )


def span(step, size, sending):
    if step == 0:
        return pl.ds(H, size)
    if sending:
        return pl.ds(H if step < 0 else size, H)
    return pl.ds(0 if step < 0 else size + H, H)


class Halo:
    def __init__(self, me, ext, sems, plane):
        self.me = me
        self.copies = []
        for i, (a, b) in enumerate(NEAR):
            copy = remote(
                ext.at[plane, span(a, TR, True), span(b, TC, True)],
                ext.at[plane, span(-a, TR, False), span(-b, TC, False)],
                sems,
                plane * 8 + i,
                me.near(a, b),
            )
            self.copies.append((a, b, copy))

    def clear(self, ext, plane):
        for a, b in NEAR:

            @pl.when(jnp.logical_not(self.me.has(a, b)))
            def _():
                part = (plane, span(a, TR, False), span(b, TC, False))
                ext[part] = jnp.zeros(ext.at[part].shape, ext.dtype)

    def start(self):
        for a, b, copy in self.copies:
            pl.when(self.me.has(a, b))(copy.start)

    def wait(self):
        for a, b, copy in self.copies:
            pl.when(self.me.has(-a, -b))(copy.wait_recv)
        for a, b, copy in self.copies:
            pl.when(self.me.has(a, b))(copy.wait_send)


def halo_body(tile, ext, sems):
    me = Place()
    halos = [Halo(me, ext, sems, plane) for plane in range(2)]
    for plane in range(2):
        ext[plane, H : H + TR, H : H + TC] = tile[plane].astype(BF16)
        halos[plane].clear(ext, plane)
    greet(me, False)
    for halo in halos:
        halo.start()
    for halo in halos:
        halo.wait()


def first_halo(tile):
    return pl.pallas_call(
        halo_body,
        out_shape=jax.ShapeDtypeStruct((2, ER, EC), BF16),
        in_specs=[pl.BlockSpec(memory_space=pltpu.VMEM)],
        out_specs=pl.BlockSpec(memory_space=pltpu.VMEM),
        scratch_shapes=[pltpu.SemaphoreType.DMA((2, 16))],
        compiler_params=pltpu.CompilerParams(
            collective_id=0, has_side_effects=True, vmem_limit_bytes=16 * MIB
        ),
        name="first_halo",
    )(tile)


class Fold:
    def __init__(self, me, axis, out, got, sems, plane):
        self.me, self.axis = me, axis
        self.copies = []
        for side, step in enumerate((-1, 1)):
            at = (step, 0) if axis == 0 else (0, step)
            copy = remote(
                out.at[side, plane], got.at[1 - side, plane], sems, plane * 2 + side, me.near(*at)
            )
            self.copies.append((step, at, copy))

    def start(self):
        for step, at, copy in self.copies:
            pl.when(self.me.has(*at))(copy.start)

    def arrive(self, add):
        for side, (step, at, copy) in enumerate(self.copies):
            back = (-at[0], -at[1])

            @pl.when(self.me.has(*back))
            def _():
                copy.wait_recv()
                add(1 - side)

    def finish(self):
        for step, at, copy in self.copies:
            pl.when(self.me.has(*at))(copy.wait_send)


def exchange_body(last, grad, probe_grad, tile, probe, *refs):
    if last:
        tile_out, probe_out = refs[:2]
        refs = refs[2:]
        ext = low_out = halo_sems = None
    else:
        tile_out, probe_out, ext, low_out = refs[:4]
        halo_sems, refs = refs[-1], refs[4:-1]
    (
        col_out, col_got, row_out, row_got, inner,
        pair_out, pair_got, plane_out, plane_got, line_out, line_got, total,
        col_sems, row_sems, pair_sems, plane_sems, line_sems,
        line_back, plane_back, pair_back,
    ) = refs
    me = Place()
    mine, others = me.c * HALF, (1 - me.c) * HALF

    for plane in range(2):
        col_out[0, plane] = grad[plane, :, :H].astype(BF16)
        col_out[1, plane] = grad[plane, :, H + TC :].astype(BF16)
    pair_out[...] = probe_grad[pl.ds(others, HALF), :].astype(BF16)
    greet(me, True)
    folds = [Fold(me, 1, col_out, col_got, col_sems, plane) for plane in range(2)]
    pair = remote(pair_out, pair_got, pair_sems, 0, me.sibling())
    pair.start()
    for fold in folds:
        fold.start()
    power = None
    for m in range(MODES):
        for part in range(2):
            start = (m * 2 + part) * S
            value = probe[start : start + S, :].astype(BF16).astype(F32)
            power = value * value if power is None else power + value * value
    scale = 1.0 / (jnp.max(power, axis=(0, 1), keepdims=True) + EPSILON)
    for plane in range(2):
        inner[plane] = grad[plane, :, H : H + TC]

    pair.wait_recv()
    plane_out[...] = (probe_grad[pl.ds(mine, HALF), :] + pair_got[...].astype(F32)).astype(BF16)
    spread = []
    for d in range(1, 16):
        other, device = me.in_plane(d)
        copy = remote(
            plane_out.at[pl.ds(pl.multiple_of(other * BLOCK, BLOCK), BLOCK)],
            plane_got.at[d - 1],
            plane_sems,
            d - 1,
            device,
        )
        copy.start()
        spread.append(copy)

    row_folds = [Fold(me, 0, row_out, row_got, row_sems, plane) for plane in range(2)]
    for plane in range(2):

        def add_cols(side, plane=plane):
            part = slice(0, H) if side == 0 else slice(TC - H, TC)
            inner[plane, :, part] += col_got[side, plane].astype(F32)

        folds[plane].arrive(add_cols)
        row_out[0, plane] = inner[plane, :H].astype(BF16)
        row_out[1, plane] = inner[plane, H + TR :].astype(BF16)
        row_folds[plane].start()

    for copy in spread:
        copy.wait_recv()
    own = plane_out[pl.ds(pl.multiple_of(me.yz * BLOCK, BLOCK), BLOCK), :].astype(F32)
    for d in range(15):
        own = own + plane_got[d].astype(F32)
    line_out[...] = own.astype(BF16)
    along = []
    for d in range(1, 4):
        other, device = me.in_line(d)
        copy = remote(
            line_out.at[pl.ds(pl.multiple_of(other * PIECE, PIECE), PIECE)],
            line_got.at[d - 1],
            line_sems,
            d - 1,
            device,
        )
        copy.start()
        along.append(copy)

    halos = []
    for plane in range(2):

        def add_rows(side, plane=plane):
            part = slice(H, S) if side == 0 else slice(TR, TR + H)
            inner[plane, part] += row_got[side, plane].astype(F32)

        row_folds[plane].arrive(add_rows)
        value = tile[plane] + inner[plane, H : H + TR] * scale
        tile_out[plane] = value
        if not last:
            ext[plane, H : H + TR, H : H + TC] = value.astype(BF16)
            halo = Halo(me, ext, halo_sems, plane)
            halo.clear(ext, plane)
            halo.start()
            halos.append(halo)

    for copy in along:
        copy.wait_recv()
    own = line_out[pl.ds(pl.multiple_of(me.x * PIECE, PIECE), PIECE), :].astype(F32)
    for d in range(3):
        own = own + line_got[d].astype(F32)
    base = me.c * HALF + me.yz * BLOCK
    piece = pl.ds(pl.multiple_of(base + me.x * PIECE, PIECE), PIECE)
    total[piece, :] = own.astype(BF16)
    backs = []
    for d in range(1, 4):
        copy = remote(total.at[piece], total.at[piece], line_back, d - 1, me.in_line(d)[1])
        copy.start()
        backs.append(copy)
    for copy in backs:
        copy.wait_recv()
    block = pl.ds(pl.multiple_of(base, BLOCK), BLOCK)
    wide = []
    for d in range(1, 16):
        copy = remote(total.at[block], total.at[block], plane_back, d - 1, me.in_plane(d)[1])
        copy.start()
        wide.append(copy)
    for copy in wide:
        copy.wait_recv()
    half = pl.ds(pl.multiple_of(me.c * HALF, HALF), HALF)
    twin = remote(total.at[half], total.at[half], pair_back, 0, me.sibling())
    twin.start()

    def renew(start):
        part = (pl.ds(start, HALF), slice(None))
        value = probe[part] + total[part].astype(F32) / (COUNT * 128)
        probe_out[part] = value
        if not last:
            low_out[part] = value.astype(BF16)

    renew(mine)
    twin.wait_recv()
    renew(others)
    for halo in halos:
        halo.wait()
    for copy in [pair, *spread, *along, *backs, *wide, twin]:
        copy.wait_send()
    for fold in folds + row_folds:
        fold.finish()


def exchange(last, grad, probe_grad, tile, probe):
    sizes = [((2, TR, TC), F32), ((ROWS, S), F32)]
    if not last:
        sizes += [((2, ER, EC), BF16), ((ROWS, S), BF16)]
    vmem = pl.BlockSpec(memory_space=pltpu.VMEM)
    dma = pltpu.SemaphoreType.DMA
    scratch = [
        pltpu.VMEM((2, 2, ER, H), BF16),
        pltpu.VMEM((2, 2, ER, H), BF16),
        pltpu.VMEM((2, 2, H, TC), BF16),
        pltpu.VMEM((2, 2, H, TC), BF16),
        pltpu.VMEM((2, ER, TC), F32),
        pltpu.VMEM((HALF, S), BF16),
        pltpu.VMEM((HALF, S), BF16),
        pltpu.VMEM((HALF, S), BF16),
        pltpu.VMEM((15, BLOCK, S), BF16),
        pltpu.VMEM((BLOCK, S), BF16),
        pltpu.VMEM((3, PIECE, S), BF16),
        pltpu.VMEM((ROWS, S), BF16),
        dma((2, 4)),
        dma((2, 4)),
        dma((2, 1)),
        dma((2, 15)),
        dma((2, 3)),
        dma((2, 3)),
        dma((2, 15)),
        dma((2, 1)),
    ]
    if not last:
        scratch.append(dma((2, 16)))
    return pl.pallas_call(
        functools.partial(exchange_body, last),
        out_shape=[jax.ShapeDtypeStruct(*size) for size in sizes],
        in_specs=[vmem] * 4,
        out_specs=[vmem] * len(sizes),
        scratch_shapes=scratch,
        compiler_params=pltpu.CompilerParams(
            collective_id=2 if last else 1, has_side_effects=True, vmem_limit_bytes=40 * MIB
        ),
        name="last_exchange" if last else "exchange",
    )(grad, probe_grad.reshape(ROWS, S), tile, probe)


def shards(object_field, probe_modes, amplitude, offsets):
    dp = lax.axis_index(AXES[:2])
    obj = lax.axis_index(AXES[2:])
    offs = offsets + H - jnp.stack([dp * TR, obj * TC]).astype(jnp.int32)
    probe = probe_modes.reshape(ROWS, S)
    tile = object_field
    ext = first_halo(tile)
    low = probe.astype(BF16)
    for turn in range(ITERS):
        grad, probe_grad = propagate(offs, ext, low.reshape(MODES, 2, S, S), amplitude)
        last = turn + 1 == ITERS
        results = exchange(last, grad, probe_grad, tile, probe)
        if last:
            tile, probe = results
        else:
            tile, probe, ext, low = results
    return tile, probe.reshape(MODES, 2, S, S)


def solution(mesh):
    split = Mesh(mesh.devices.reshape(4, 4, 4, 2), AXES)
    return jax.shard_map(
        shards,
        mesh=split,
        in_specs=(
            P(None, AXES[:2], AXES[2:]),
            P(),
            P(AXES, None, None),
            P(AXES, None),
        ),
        out_specs=(P(None, AXES[:2], AXES[2:]), P()),
        check_vma=False,
    )
```

```python
import functools

import jax
import jax.numpy as jnp
import ml_dtypes
import numpy as np
from jax import lax
from jax.experimental import pallas as pl
from jax.experimental.pallas import tpu as pltpu
from jax.sharding import Mesh
from jax.sharding import PartitionSpec as P

ITERS = 2
AXES = ("dp_0", "dp_1", "obj_0", "obj_1")
EPSILON = 1e-06
F32, BF16 = jnp.float32, jnp.bfloat16
S = 256
H = S // 2
TR, TC = 256, 512
ER, EC = TR + S, TC + S
MODES, COUNT = 4, 6
ROWS = MODES * 2 * S
CHUNKS = 2
CHUNK = ROWS // CHUNKS
HALF, BLOCK = CHUNK // 2, CHUNK // 32
ORDER = (
    "line0",
    "line1",
    "back0",
    "back1",
    "rows0",
    "rows1",
    "twin0",
    "own0",
    "twin1",
    "own1",
    "rest0",
    "rest1",
)
MIB = 1 << 20


def dft_tables():
    counter = np.arange(S)
    angle = 2.0 * np.pi * (counter[:, None] * counter[None, :] % S) / S
    re = (np.cos(angle) / 16.0).astype(np.float32).astype(ml_dtypes.bfloat16)
    im = (-np.sin(angle) / 16.0).astype(np.float32).astype(ml_dtypes.bfloat16)
    return np.block([[re, -im], [im, re]]), np.block([[re, im], [-im, re]])


def propagate_body(
    offs, ext, probe_in, amp, plus, minus, grad, probe_grad, ext32, probe, patch, wave, half, far
):
    n = pl.program_id(0)

    def by_rows(ref, value):
        @pl.loop(0, ref.shape[0] // 64)
        def _(i):
            rows = pl.ds(i * 64, 64)
            ref[rows] = value(rows)

    @pl.when(n == 0)
    def _():
        for p in range(2):
            by_rows(grad.at[p], lambda rows: jnp.zeros((64, EC), F32))
            by_rows(ext32.at[p], lambda rows: ext[p, rows].astype(F32))
            for m in range(MODES):
                by_rows(probe_grad.at[m, p], lambda rows: jnp.zeros((64, S), F32))
                by_rows(
                    probe.at[m, p], lambda rows: probe_in[m, p, rows].astype(BF16).astype(F32)
                )

    row, col = offs[n, 0], offs[n, 1]
    row_base = pl.multiple_of((row // 8) * 8, 8)
    row_shift = row - row_base
    col_block = col // 128
    shift = col - col_block * 128
    rows = pl.ds(row_base, S + 8)

    def cols(i):
        return pl.ds(pl.multiple_of((col_block + i) * 128, 128), 128)

    lane = lax.broadcasted_iota(jnp.int32, (S + 8, 128), 1)
    for p in range(2):
        x = [pltpu.roll(ext32[p, rows, cols(i)], lax.rem(128 - shift, 128), 1) for i in range(3)]
        for i in range(2):
            joined = jnp.where(lane < 128 - shift, x[i], x[i + 1])
            joined = pltpu.roll(joined, lax.rem(S + 8 - row_shift, S + 8), 0)
            patch[p, :, i * 128 : (i + 1) * 128] = joined[:S]
    for m in range(MODES):
        qr, qi = probe[m, 0], probe[m, 1]
        pr, pi = patch[0], patch[1]
        wave[m, :S, :] = (qr * pr - qi * pi).astype(BF16)
        wave[m, S:, :] = (qr * pi + qi * pr).astype(BF16)
        mid = jnp.dot(plus[...], wave[m], preferred_element_type=F32).astype(BF16)
        half[m * S : (m + 1) * S, :S] = mid[:S]
        half[m * S : (m + 1) * S, S:] = mid[S:]
    far[...] = jnp.dot(half[...], minus[...], preferred_element_type=F32)
    intensity = None
    for m in range(MODES):
        fr, fi = far[m * S : (m + 1) * S, :S], far[m * S : (m + 1) * S, S:]
        term = fr * fr + fi * fi
        intensity = term if intensity is None else intensity + term
    ratio = amp[0] * jnp.minimum(lax.rsqrt(intensity), 1.0) - 1.0
    for m in range(MODES):
        wave[m, :S, :] = (far[m * S : (m + 1) * S, :S] * ratio).astype(BF16)
        wave[m, S:, :] = (far[m * S : (m + 1) * S, S:] * ratio).astype(BF16)
        mid = jnp.dot(minus[...], wave[m], preferred_element_type=F32).astype(BF16)
        half[m * S : (m + 1) * S, :S] = mid[:S]
        half[m * S : (m + 1) * S, S:] = mid[S:]
    far[...] = jnp.dot(half[...], plus[...], preferred_element_type=F32)
    gr = gi = None
    for m in range(MODES):
        cr, ci = far[m * S : (m + 1) * S, :S], far[m * S : (m + 1) * S, S:]
        qr, qi = probe[m, 0], probe[m, 1]
        a, b = qr * cr + qi * ci, qr * ci - qi * cr
        gr = a if gr is None else gr + a
        gi = b if gi is None else gi + b
        pr, pi = patch[0], patch[1]
        probe_grad[m, 0] += pr * cr + pi * ci
        probe_grad[m, 1] += pr * ci - pi * cr
    for p, value in enumerate((gr, gi)):
        value = jnp.concatenate([value, jnp.zeros((8, S), F32)], 0)
        x = [
            pltpu.roll(pltpu.roll(value[:, i * 128 : (i + 1) * 128], row_shift, 0), shift, 1)
            for i in range(2)
        ]
        zero = jnp.zeros_like(x[0])
        parts = (
            jnp.where(lane >= shift, x[0], zero),
            jnp.where(lane >= shift, x[1], x[0]),
            jnp.where(lane >= shift, zero, x[1]),
        )
        for i in range(3):
            grad[p, rows, cols(i)] += parts[i]


def propagate(offs, ext, probe, amplitude):
    plus, minus = dft_tables()

    def whole(*shape):
        return pl.BlockSpec(shape, lambda n, o: (0,) * len(shape))

    return pl.pallas_call(
        propagate_body,
        grid_spec=pltpu.PrefetchScalarGridSpec(
            num_scalar_prefetch=1,
            grid=(COUNT,),
            in_specs=[
                whole(2, ER, EC),
                whole(MODES, 2, S, S),
                pl.BlockSpec((1, S, S), lambda n, o: (n, 0, 0)),
                whole(2 * S, 2 * S),
                whole(2 * S, 2 * S),
            ],
            out_specs=[whole(2, ER, EC), whole(MODES, 2, S, S)],
            scratch_shapes=[
                pltpu.VMEM((2, ER, EC), F32),
                pltpu.VMEM((MODES, 2, S, S), F32),
                pltpu.VMEM((2, S, S), F32),
                pltpu.VMEM((MODES, 2 * S, S), BF16),
                pltpu.VMEM((MODES * S, 2 * S), BF16),
                pltpu.VMEM((MODES * S, 2 * S), F32),
            ],
        ),
        out_shape=[
            jax.ShapeDtypeStruct((2, ER, EC), F32),
            jax.ShapeDtypeStruct((MODES, 2, S, S), F32),
        ],
        compiler_params=pltpu.CompilerParams(
            dimension_semantics=("arbitrary",), vmem_limit_bytes=32 * MIB
        ),
        name="propagate",
    )(offs, ext, probe, amplitude, jnp.asarray(plus), jnp.asarray(minus))


NEAR = [(a, b) for a in (-1, 0, 1) for b in (-1, 0, 1) if (a, b) != (0, 0)]


class Place:
    def __init__(self):
        self.z, self.x, self.y, self.c = (lax.axis_index(name) for name in AXES)
        self.dp = self.z * 4 + self.x
        self.obj = self.y * 2 + self.c
        self.yz = self.y * 4 + self.z

    def has(self, a, b):
        found = None
        for step, place, count in ((a, self.dp, 16), (b, self.obj, 8)):
            if step:
                test = place > 0 if step < 0 else place < count - 1
                found = test if found is None else jnp.logical_and(found, test)
        return found

    def near(self, a, b):
        dp, obj = self.dp + a, self.obj + b
        return (dp // 4, dp % 4, obj // 2, obj % 2)

    def sibling(self):
        return (self.z, self.x, self.y, 1 - self.c)

    def in_plane(self, d):
        other = (self.yz + d) % 16
        return other, (other % 4, self.x, other // 4, self.c)

    def in_line(self, d):
        other = (self.x + d) % 4
        return other, (self.z, other, self.y, self.c)


def signal_all(me, everyone):
    barrier = pltpu.get_barrier_semaphore()
    expected = jnp.int32(0)
    for a, b in NEAR:
        there = me.has(a, b)

        @pl.when(there)
        def _():
            pl.semaphore_signal(
                barrier, inc=1, device_id=me.near(a, b), device_id_type=pl.DeviceIdType.MESH
            )

        expected = expected + there.astype(jnp.int32)
    if everyone:
        others = [me.sibling()]
        others += [me.in_plane(d)[1] for d in range(1, 16)]
        others += [me.in_line(d)[1] for d in range(1, 4)]
        for other in others:
            pl.semaphore_signal(
                barrier, inc=1, device_id=other, device_id_type=pl.DeviceIdType.MESH
            )
        expected = expected + len(others)
    return expected


def wait_all(expected):
    pl.semaphore_wait(pltpu.get_barrier_semaphore(), expected)


def remote(src, dst, sems, index, device):
    return pltpu.make_async_remote_copy(
        src_ref=src,
        dst_ref=dst,
        send_sem=sems.at[0, index],
        recv_sem=sems.at[1, index],
        device_id=device,
        device_id_type=pl.DeviceIdType.MESH,
    )


def span(step, size, sending):
    if step == 0:
        return pl.ds(H, size)
    if sending:
        return pl.ds(H if step < 0 else size, H)
    return pl.ds(0 if step < 0 else size + H, H)


class Halo:
    def __init__(self, me, ext, sems, plane):
        self.me = me
        self.copies = []
        for i, (a, b) in enumerate(NEAR):
            copy = remote(
                ext.at[plane, span(a, TR, True), span(b, TC, True)],
                ext.at[plane, span(-a, TR, False), span(-b, TC, False)],
                sems,
                plane * 8 + i,
                me.near(a, b),
            )
            self.copies.append((a, b, copy))

    def clear(self, ext, plane):
        for a, b in NEAR:

            @pl.when(jnp.logical_not(self.me.has(a, b)))
            def _():
                part = (plane, span(a, TR, False), span(b, TC, False))
                ext[part] = jnp.zeros(ext.at[part].shape, ext.dtype)

    def start(self):
        for a, b, copy in self.copies:
            pl.when(self.me.has(a, b))(copy.start)

    def wait(self):
        for a, b, copy in self.copies:
            pl.when(self.me.has(-a, -b))(copy.wait_recv)
        for a, b, copy in self.copies:
            pl.when(self.me.has(a, b))(copy.wait_send)


def halo_body(tile, ext, sems):
    me = Place()
    expected = signal_all(me, False)
    halos = [Halo(me, ext, sems, plane) for plane in range(2)]
    for plane in range(2):
        ext[plane, H : H + TR, H : H + TC] = tile[plane].astype(BF16)
        halos[plane].clear(ext, plane)
    wait_all(expected)
    for halo in halos:
        halo.start()
    for halo in halos:
        halo.wait()


def first_halo(tile):
    return pl.pallas_call(
        halo_body,
        out_shape=jax.ShapeDtypeStruct((2, ER, EC), BF16),
        in_specs=[pl.BlockSpec(memory_space=pltpu.VMEM)],
        out_specs=pl.BlockSpec(memory_space=pltpu.VMEM),
        scratch_shapes=[pltpu.SemaphoreType.DMA((2, 16))],
        compiler_params=pltpu.CompilerParams(
            collective_id=0, has_side_effects=True, vmem_limit_bytes=16 * MIB
        ),
        name="first_halo",
    )(tile)


class Fold:
    def __init__(self, me, axis, out, got, sems, plane):
        self.me, self.axis = me, axis
        self.copies = []
        for side, step in enumerate((-1, 1)):
            at = (step, 0) if axis == 0 else (0, step)
            copy = remote(
                out.at[side, plane], got.at[1 - side, plane], sems, plane * 2 + side, me.near(*at)
            )
            self.copies.append((step, at, copy))

    def start(self):
        for step, at, copy in self.copies:
            pl.when(self.me.has(*at))(copy.start)

    def arrive(self, add):
        for side, (step, at, copy) in enumerate(self.copies):
            back = (-at[0], -at[1])

            @pl.when(self.me.has(*back))
            def _():
                copy.wait_recv()
                add(1 - side)

    def finish(self):
        for step, at, copy in self.copies:
            pl.when(self.me.has(*at))(copy.wait_send)


class Probe:
    def __init__(self, me, chunk, probe_grad, total, bufs, sems):
        self.me, self.chunk, self.source, self.total = me, chunk, probe_grad, total
        self.pair_out, self.pair_got, self.plane_out, self.plane_got, self.line_got = (
            buf.at[chunk] for buf in bufs
        )
        self.pair_sems, self.plane_sems, self.line_sems, self.back_sems, self.twin_sems = sems
        start = chunk * CHUNK
        self.mine = pl.multiple_of(start + me.c * HALF, HALF)
        self.others = pl.multiple_of(start + (1 - me.c) * HALF, HALF)
        self.sent = []

    def go(self, copies):
        for copy in copies:
            copy.start()
        self.sent += copies
        return copies

    def cast(self):
        self.pair_out[...] = self.source[pl.ds(self.others, HALF), :].astype(BF16)

    def pair(self):
        self.pairs = self.go(
            [remote(self.pair_out, self.pair_got, self.pair_sems, self.chunk, self.me.sibling())]
        )

    def plane(self):
        self.pairs[0].wait_recv()
        own = self.source[pl.ds(self.mine, HALF), :]
        self.plane_out[...] = (own + self.pair_got[...].astype(F32)).astype(BF16)
        copies = []
        for d in range(1, 16):
            other, device = self.me.in_plane(d)
            copies.append(
                remote(
                    self.plane_out.at[pl.ds(pl.multiple_of(other * BLOCK, BLOCK), BLOCK)],
                    self.plane_got.at[d - 1],
                    self.plane_sems,
                    self.chunk * 15 + d - 1,
                    device,
                )
            )
        self.planes = self.go(copies)

    def line(self):
        for copy in self.planes:
            copy.wait_recv()
        own = self.plane_out[pl.ds(pl.multiple_of(self.me.yz * BLOCK, BLOCK), BLOCK), :].astype(F32)
        for d in range(15):
            own = own + self.plane_got[d].astype(F32)
        slot = self.line_got.at[self.me.x]
        slot[...] = own.astype(BF16)
        self.lines = self.go(
            [
                remote(slot, slot, self.line_sems, self.chunk * 3 + d - 1, self.me.in_line(d)[1])
                for d in range(1, 4)
            ]
        )

    def back(self):
        for copy in self.lines:
            copy.wait_recv()
        value = self.line_got[0].astype(F32)
        for d in range(1, 4):
            value = value + self.line_got[d].astype(F32)
        start = pl.multiple_of(self.mine + self.me.yz * BLOCK, BLOCK)
        block = self.total.at[pl.ds(start, BLOCK)]
        block[...] = value.astype(BF16)
        self.backs = self.go(
            [
                remote(block, block, self.back_sems, self.chunk * 15 + d - 1, self.me.in_plane(d)[1])
                for d in range(1, 16)
            ]
        )

    def twin(self):
        for copy in self.backs:
            copy.wait_recv()
        half = self.total.at[pl.ds(self.mine, HALF)]
        self.twins = self.go([remote(half, half, self.twin_sems, self.chunk, self.me.sibling())])

    def renew(self, own, probe, probe_out):
        if not own:
            self.twins[0].wait_recv()
        if probe_out is None:
            return
        part = (pl.ds(self.mine if own else self.others, HALF), slice(None))
        value = probe[part] + self.total[part].astype(F32) / (COUNT * 128)
        probe_out[part] = value

    def finish(self):
        for copy in self.sent:
            copy.wait_send()


def exchange_body(last, grad, probe_grad, tile, probe, *refs):
    if last:
        tile_out, total = refs[:2]
        refs = refs[2:]
        ext = probe_out = halo_sems = None
    else:
        tile_out, probe_out, ext = refs[:3]
        halo_sems, total, refs = refs[-2], refs[-1], refs[3:-2]
    col_out, col_got, row_out, row_got, inner = refs[:5]
    col_sems, row_sems = refs[10:12]
    me = Place()
    expected = signal_all(me, True)
    chunks = [Probe(me, i, probe_grad, total, refs[5:10], refs[12:]) for i in range(CHUNKS)]
    for chunk in chunks:
        chunk.cast()
    for plane in range(2):
        col_out[0, plane] = grad[plane, :, :H].astype(BF16)
        col_out[1, plane] = grad[plane, :, H + TC :].astype(BF16)
    wait_all(expected)
    folds = [Fold(me, 1, col_out, col_got, col_sems, plane) for plane in range(2)]
    row_folds = [Fold(me, 0, row_out, row_got, row_sems, plane) for plane in range(2)]
    halos = []
    for chunk in chunks:
        chunk.pair()
    for fold in folds:
        fold.start()
    if not last:
        for plane in range(2):
            halos.append(Halo(me, ext, halo_sems, plane))
            halos[-1].clear(ext, plane)
    for plane in range(2):
        inner[plane] = grad[plane, :, H : H + TC]
    for chunk in chunks:
        chunk.plane()

    def fold_cols(plane):
        def add(side):
            part = slice(0, H) if side == 0 else slice(TC - H, TC)
            inner[plane, :, part] += col_got[side, plane].astype(F32)

        folds[plane].arrive(add)
        row_out[0, plane] = inner[plane, :H].astype(BF16)
        row_out[1, plane] = inner[plane, H + TR :].astype(BF16)
        row_folds[plane].start()

    for plane in range(2):
        fold_cols(plane)
    power = None
    for m in range(MODES):
        for part in range(2):
            start = (m * 2 + part) * S
            value = probe[start : start + S, :].astype(BF16).astype(F32)
            power = value * value if power is None else power + value * value
    scale = 1.0 / (jnp.max(power, axis=(0, 1), keepdims=True) + EPSILON)

    def fold_rows(plane):
        def add(side):
            part = slice(H, S) if side == 0 else slice(TR, TR + H)
            inner[plane, part] += row_got[side, plane].astype(F32)

        row_folds[plane].arrive(add)
        value = inner[plane, H : H + TR] * scale
        if last:
            tile_out[plane] = value
        else:
            value = tile[plane] + value
            tile_out[plane] = value
            ext[plane, H : H + TR, H : H + TC] = value.astype(BF16)
            halos[plane].start()

    for step in ORDER:
        kind, index = step[:-1], int(step[-1])
        if kind == "rows":
            fold_rows(index)
        elif kind in ("line", "back", "twin"):
            if index < CHUNKS:
                getattr(chunks[index], kind)()
        elif kind == "own" and index < CHUNKS:
            chunks[index].renew(True, probe, probe_out)
        elif kind == "rest" and index < CHUNKS:
            chunks[index].renew(False, probe, probe_out)
    for halo in halos:
        halo.wait()
    for chunk in chunks:
        chunk.finish()
    for fold in folds + row_folds:
        fold.finish()


def exchange(last, grad, probe_grad, tile, probe):
    sizes = [((2, TR, TC), F32), ((ROWS, S), BF16 if last else F32)]
    if not last:
        sizes += [((2, ER, EC), BF16)]
    vmem = pl.BlockSpec(memory_space=pltpu.VMEM)
    dma = pltpu.SemaphoreType.DMA
    scratch = [
        pltpu.VMEM((2, 2, ER, H), BF16),
        pltpu.VMEM((2, 2, ER, H), BF16),
        pltpu.VMEM((2, 2, H, TC), BF16),
        pltpu.VMEM((2, 2, H, TC), BF16),
        pltpu.VMEM((2, ER, TC), F32),
        pltpu.VMEM((CHUNKS, HALF, S), BF16),
        pltpu.VMEM((CHUNKS, HALF, S), BF16),
        pltpu.VMEM((CHUNKS, HALF, S), BF16),
        pltpu.VMEM((CHUNKS, 15, BLOCK, S), BF16),
        pltpu.VMEM((CHUNKS, 4, BLOCK, S), BF16),
        dma((2, 4)),
        dma((2, 4)),
        dma((2, CHUNKS)),
        dma((2, 15 * CHUNKS)),
        dma((2, 3 * CHUNKS)),
        dma((2, 15 * CHUNKS)),
        dma((2, CHUNKS)),
    ]
    if not last:
        scratch += [dma((2, 16)), pltpu.VMEM((ROWS, S), BF16)]
    return pl.pallas_call(
        functools.partial(exchange_body, last),
        out_shape=[jax.ShapeDtypeStruct(*size) for size in sizes],
        in_specs=[vmem] * 4,
        out_specs=[vmem] * len(sizes),
        scratch_shapes=scratch,
        compiler_params=pltpu.CompilerParams(
            collective_id=2 if last else 1, has_side_effects=True, vmem_limit_bytes=40 * MIB
        ),
        name="last_exchange" if last else "exchange",
    )(grad, probe_grad.reshape(ROWS, S), tile, probe)


def shards(object_field, probe_modes, amplitude, offsets):
    dp = lax.axis_index(AXES[:2])
    obj = lax.axis_index(AXES[2:])
    offs = offsets + H - jnp.stack([dp * TR, obj * TC]).astype(jnp.int32)
    probe = probe_modes.reshape(ROWS, S)
    tile = object_field
    ext = first_halo(tile)
    for turn in range(ITERS):
        grad, probe_grad = propagate(offs, ext, probe.reshape(MODES, 2, S, S), amplitude)
        last = turn + 1 == ITERS
        results = exchange(last, grad, probe_grad, tile, probe)
        if last:
            tile = tile + results[0]
            probe = probe + results[1].astype(F32) / (COUNT * 128)
        else:
            tile, probe, ext = results
    return tile, probe.reshape(MODES, 2, S, S)


def solution(mesh):
    split = Mesh(mesh.devices.reshape(4, 4, 4, 2), AXES)
    return jax.shard_map(
        shards,
        mesh=split,
        in_specs=(
            P(None, AXES[:2], AXES[2:]),
            P(),
            P(AXES, None, None),
            P(AXES, None),
        ),
        out_specs=(P(None, AXES[:2], AXES[2:]), P()),
        check_vma=False,
    )
```

```python
import functools

import jax
import jax.numpy as jnp
import ml_dtypes
import numpy as np
from jax import lax
from jax.experimental import pallas as pl
from jax.experimental.pallas import tpu as pltpu
from jax.sharding import Mesh
from jax.sharding import PartitionSpec as P

ITERS = 2
AXES = ("dp_0", "dp_1", "obj_0", "obj_1")
EPSILON = 1e-06
F32, BF16 = jnp.float32, jnp.bfloat16
S = 256
H = S // 2
TR, TC = 256, 512
ER, EC = TR + S, TC + S
MODES, COUNT = 4, 6
GROUP = 3
ROWS = MODES * 2 * S
CHUNKS = 2
CHUNK = ROWS // CHUNKS
HALF, BLOCK = CHUNK // 2, CHUNK // 32
ORDER = (
    "line0",
    "line1",
    "back0",
    "back1",
    "rows0",
    "rows1",
    "twin0",
    "own0",
    "twin1",
    "own1",
    "rest0",
    "rest1",
)
MIB = 1 << 20


def dft_tables():
    counter = np.arange(S)
    angle = 2.0 * np.pi * (counter[:, None] * counter[None, :] % S) / S
    re = (np.cos(angle) / 16.0).astype(np.float32).astype(ml_dtypes.bfloat16)
    im = (-np.sin(angle) / 16.0).astype(np.float32).astype(ml_dtypes.bfloat16)
    return np.block([[re, -im], [im, re]]), np.block([[re, im], [-im, re]])


def propagate_body(
    offs, ext, probe_in, amp, plus, minus, grad, probe_grad,
    ext32, probe, patches, waves, halves, fars,
):
    turn = pl.program_id(0)
    me = Place()

    def by_rows(ref, value):
        @pl.loop(0, ref.shape[0] // 64)
        def _(i):
            rows = pl.ds(i * 64, 64)
            ref[rows] = value(rows)

    @pl.when(turn == 0)
    def _():
        for p in range(2):
            by_rows(grad.at[p], lambda rows: jnp.zeros((64, EC), F32))
            by_rows(ext32.at[p], lambda rows: ext[p, rows].astype(F32))
            for m in range(MODES):
                by_rows(probe_grad.at[m, p], lambda rows: jnp.zeros((64, S), F32))
                by_rows(
                    probe.at[m, p], lambda rows: probe_in[m, p, rows].astype(BF16).astype(F32)
                )

    lane = lax.broadcasted_iota(jnp.int32, (S + 8, 128), 1)

    def place(a):
        row = offs[0, turn * GROUP + a] - me.dp * TR + H
        col = offs[1, turn * GROUP + a] - me.obj * TC + H
        row_base = pl.multiple_of((row // 8) * 8, 8)
        col_block = col // 128

        def cols(i):
            return pl.ds(pl.multiple_of((col_block + i) * 128, 128), 128)

        return pl.ds(row_base, S + 8), row - row_base, cols, col - col_block * 128

    def left(table, wave, half, m):
        mid = jnp.dot(table[...], wave[m], preferred_element_type=F32).astype(BF16)
        half[m * S : (m + 1) * S, :S] = mid[:S]
        half[m * S : (m + 1) * S, S:] = mid[S:]

    def forward(a):
        patch, wave, half, far = patches.at[a], waves.at[a], halves.at[a], fars.at[a]
        rows, row_shift, cols, shift = place(a)
        for p in range(2):
            x = [
                pltpu.roll(ext32[p, rows, cols(i)], lax.rem(128 - shift, 128), 1) for i in range(3)
            ]
            for i in range(2):
                joined = jnp.where(lane < 128 - shift, x[i], x[i + 1])
                joined = pltpu.roll(joined, lax.rem(S + 8 - row_shift, S + 8), 0)
                patch[p, :, i * 128 : (i + 1) * 128] = joined[:S]
        for m in range(MODES):
            qr, qi = probe[m, 0], probe[m, 1]
            pr, pi = patch[0], patch[1]
            wave[m, :S, :] = (qr * pr - qi * pi).astype(BF16)
            wave[m, S:, :] = (qr * pi + qi * pr).astype(BF16)
            left(plus, wave, half, m)
        far[...] = jnp.dot(half[...], minus[...], preferred_element_type=F32)

    def backward(a):
        patch, wave, half, far = patches.at[a], waves.at[a], halves.at[a], fars.at[a]
        rows, row_shift, cols, shift = place(a)
        intensity = None
        for m in range(MODES):
            fr, fi = far[m * S : (m + 1) * S, :S], far[m * S : (m + 1) * S, S:]
            term = fr * fr + fi * fi
            intensity = term if intensity is None else intensity + term
        ratio = amp[a] * jnp.minimum(lax.rsqrt(intensity), 1.0) - 1.0
        for m in range(MODES):
            wave[m, :S, :] = (far[m * S : (m + 1) * S, :S] * ratio).astype(BF16)
            wave[m, S:, :] = (far[m * S : (m + 1) * S, S:] * ratio).astype(BF16)
            left(minus, wave, half, m)
        far[...] = jnp.dot(half[...], plus[...], preferred_element_type=F32)
        gr = gi = None
        for m in range(MODES):
            cr, ci = far[m * S : (m + 1) * S, :S], far[m * S : (m + 1) * S, S:]
            qr, qi = probe[m, 0], probe[m, 1]
            to_re, to_im = qr * cr + qi * ci, qr * ci - qi * cr
            gr = to_re if gr is None else gr + to_re
            gi = to_im if gi is None else gi + to_im
            pr, pi = patch[0], patch[1]
            probe_grad[m, 0] += pr * cr + pi * ci
            probe_grad[m, 1] += pr * ci - pi * cr
        for p, value in enumerate((gr, gi)):
            value = jnp.concatenate([value, jnp.zeros((8, S), F32)], 0)
            x = [
                pltpu.roll(pltpu.roll(value[:, i * 128 : (i + 1) * 128], row_shift, 0), shift, 1)
                for i in range(2)
            ]
            zero = jnp.zeros_like(x[0])
            parts = (
                jnp.where(lane >= shift, x[0], zero),
                jnp.where(lane >= shift, x[1], x[0]),
                jnp.where(lane >= shift, zero, x[1]),
            )
            for i in range(3):
                grad[p, rows, cols(i)] += parts[i]

    for a in range(GROUP):
        forward(a)
    for a in range(GROUP):
        backward(a)


def propagate(offs, ext, probe, amplitude):
    plus, minus = dft_tables()

    def whole(*shape):
        return pl.BlockSpec(shape, lambda n, o: (0,) * len(shape))

    return pl.pallas_call(
        propagate_body,
        grid_spec=pltpu.PrefetchScalarGridSpec(
            num_scalar_prefetch=1,
            grid=(COUNT // GROUP,),
            in_specs=[
                whole(2, ER, EC),
                whole(MODES, 2, S, S),
                pl.BlockSpec((GROUP, S, S), lambda n, o: (n, 0, 0)),
                whole(2 * S, 2 * S),
                whole(2 * S, 2 * S),
            ],
            out_specs=[whole(2, ER, EC), whole(MODES, 2, S, S)],
            scratch_shapes=[
                pltpu.VMEM((2, ER, EC), F32),
                pltpu.VMEM((MODES, 2, S, S), F32),
                pltpu.VMEM((GROUP, 2, S, S), F32),
                pltpu.VMEM((GROUP, MODES, 2 * S, S), BF16),
                pltpu.VMEM((GROUP, MODES * S, 2 * S), BF16),
                pltpu.VMEM((GROUP, MODES * S, 2 * S), F32),
            ],
        ),
        out_shape=[
            jax.ShapeDtypeStruct((2, ER, EC), F32),
            jax.ShapeDtypeStruct((MODES, 2, S, S), F32),
        ],
        compiler_params=pltpu.CompilerParams(
            dimension_semantics=("arbitrary",), vmem_limit_bytes=36 * MIB
        ),
        name="propagate",
    )(offs, ext, probe, amplitude, jnp.asarray(plus), jnp.asarray(minus))


NEAR = [(a, b) for a in (-1, 0, 1) for b in (-1, 0, 1) if (a, b) != (0, 0)]


class Place:
    def __init__(self):
        self.z, self.x, self.y, self.c = (lax.axis_index(name) for name in AXES)
        self.dp = self.z * 4 + self.x
        self.obj = self.y * 2 + self.c
        self.yz = self.y * 4 + self.z

    def has(self, a, b):
        found = None
        for step, place, count in ((a, self.dp, 16), (b, self.obj, 8)):
            if step:
                test = place > 0 if step < 0 else place < count - 1
                found = test if found is None else jnp.logical_and(found, test)
        return found

    def near(self, a, b):
        dp, obj = self.dp + a, self.obj + b
        return (dp // 4, dp % 4, obj // 2, obj % 2)

    def sibling(self):
        return (self.z, self.x, self.y, 1 - self.c)

    def in_plane(self, d):
        other = (self.yz + d) % 16
        return other, (other % 4, self.x, other // 4, self.c)

    def in_line(self, d):
        other = (self.x + d) % 4
        return other, (self.z, other, self.y, self.c)


def signal_all(me, everyone):
    barrier = pltpu.get_barrier_semaphore()
    expected = jnp.int32(0)
    for a, b in NEAR:
        there = me.has(a, b)

        @pl.when(there)
        def _():
            pl.semaphore_signal(
                barrier, inc=1, device_id=me.near(a, b), device_id_type=pl.DeviceIdType.MESH
            )

        expected = expected + there.astype(jnp.int32)
    if everyone:
        others = [me.sibling()]
        others += [me.in_plane(d)[1] for d in range(1, 16)]
        others += [me.in_line(d)[1] for d in range(1, 4)]
        for other in others:
            pl.semaphore_signal(
                barrier, inc=1, device_id=other, device_id_type=pl.DeviceIdType.MESH
            )
        expected = expected + len(others)
    return expected


def wait_all(expected):
    pl.semaphore_wait(pltpu.get_barrier_semaphore(), expected)


def remote(src, dst, sems, index, device):
    return pltpu.make_async_remote_copy(
        src_ref=src,
        dst_ref=dst,
        send_sem=sems.at[0, index],
        recv_sem=sems.at[1, index],
        device_id=device,
        device_id_type=pl.DeviceIdType.MESH,
    )


def span(step, size, sending):
    if step == 0:
        return pl.ds(H, size)
    if sending:
        return pl.ds(H if step < 0 else size, H)
    return pl.ds(0 if step < 0 else size + H, H)


class Halo:
    def __init__(self, me, ext, sems, plane):
        self.me = me
        self.copies = []
        for i, (a, b) in enumerate(NEAR):
            copy = remote(
                ext.at[plane, span(a, TR, True), span(b, TC, True)],
                ext.at[plane, span(-a, TR, False), span(-b, TC, False)],
                sems,
                plane * 8 + i,
                me.near(a, b),
            )
            self.copies.append((a, b, copy))

    def clear(self, ext, plane):
        for a, b in NEAR:

            @pl.when(jnp.logical_not(self.me.has(a, b)))
            def _():
                part = (plane, span(a, TR, False), span(b, TC, False))
                ext[part] = jnp.zeros(ext.at[part].shape, ext.dtype)

    def start(self):
        for a, b, copy in self.copies:
            pl.when(self.me.has(a, b))(copy.start)

    def wait(self):
        for a, b, copy in self.copies:
            pl.when(self.me.has(-a, -b))(copy.wait_recv)
        for a, b, copy in self.copies:
            pl.when(self.me.has(a, b))(copy.wait_send)


def halo_body(tile, ext, local, sems, local_sems):
    me = Place()
    loads = [
        pltpu.make_async_copy(tile.at[plane], local.at[plane], local_sems.at[plane])
        for plane in range(2)
    ]
    for load in loads:
        load.start()
    expected = signal_all(me, False)
    halos = [Halo(me, ext, sems, plane) for plane in range(2)]
    for plane in range(2):
        halos[plane].clear(ext, plane)
    for plane in range(2):
        loads[plane].wait()
        ext[plane, H : H + TR, H : H + TC] = local[plane].astype(BF16)
    wait_all(expected)
    for halo in halos:
        halo.start()
    for halo in halos:
        halo.wait()


def first_halo(tile):
    return pl.pallas_call(
        halo_body,
        out_shape=jax.ShapeDtypeStruct((2, ER, EC), BF16),
        in_specs=[pl.BlockSpec(memory_space=pltpu.HBM)],
        out_specs=pl.BlockSpec(memory_space=pltpu.VMEM),
        scratch_shapes=[
            pltpu.VMEM((2, TR, TC), F32),
            pltpu.SemaphoreType.DMA((2, 16)),
            pltpu.SemaphoreType.DMA((2,)),
        ],
        compiler_params=pltpu.CompilerParams(
            collective_id=0, has_side_effects=True, vmem_limit_bytes=16 * MIB
        ),
        name="first_halo",
    )(tile)


class Fold:
    def __init__(self, me, axis, out, got, sems, plane):
        self.me, self.axis = me, axis
        self.copies = []
        for side, step in enumerate((-1, 1)):
            at = (step, 0) if axis == 0 else (0, step)
            copy = remote(
                out.at[side, plane], got.at[1 - side, plane], sems, plane * 2 + side, me.near(*at)
            )
            self.copies.append((step, at, copy))

    def start(self):
        for step, at, copy in self.copies:
            pl.when(self.me.has(*at))(copy.start)

    def arrive(self, add):
        for side, (step, at, copy) in enumerate(self.copies):
            back = (-at[0], -at[1])

            @pl.when(self.me.has(*back))
            def _():
                copy.wait_recv()
                add(1 - side)

    def finish(self):
        for step, at, copy in self.copies:
            pl.when(self.me.has(*at))(copy.wait_send)


class Probe:
    def __init__(self, me, chunk, probe_grad, total, bufs, sems):
        self.me, self.chunk, self.source, self.total = me, chunk, probe_grad, total
        self.pair_out, self.pair_got, self.plane_out, self.plane_got, self.line_got = (
            buf.at[chunk] for buf in bufs
        )
        self.pair_sems, self.plane_sems, self.line_sems, self.back_sems, self.twin_sems = sems
        start = chunk * CHUNK
        self.mine = pl.multiple_of(start + me.c * HALF, HALF)
        self.others = pl.multiple_of(start + (1 - me.c) * HALF, HALF)
        self.sent = []

    def go(self, copies):
        for copy in copies:
            copy.start()
        self.sent += copies
        return copies

    def cast(self):
        self.pair_out[...] = self.source[pl.ds(self.others, HALF), :].astype(BF16)

    def pair(self):
        self.pairs = self.go(
            [remote(self.pair_out, self.pair_got, self.pair_sems, self.chunk, self.me.sibling())]
        )

    def plane(self):
        self.pairs[0].wait_recv()
        own = self.source[pl.ds(self.mine, HALF), :]
        self.plane_out[...] = (own + self.pair_got[...].astype(F32)).astype(BF16)
        copies = []
        for d in range(1, 16):
            other, device = self.me.in_plane(d)
            copies.append(
                remote(
                    self.plane_out.at[pl.ds(pl.multiple_of(other * BLOCK, BLOCK), BLOCK)],
                    self.plane_got.at[d - 1],
                    self.plane_sems,
                    self.chunk * 15 + d - 1,
                    device,
                )
            )
        self.planes = self.go(copies)

    def line(self):
        for copy in self.planes:
            copy.wait_recv()
        own = self.plane_out[pl.ds(pl.multiple_of(self.me.yz * BLOCK, BLOCK), BLOCK), :].astype(F32)
        for d in range(15):
            own = own + self.plane_got[d].astype(F32)
        slot = self.line_got.at[self.me.x]
        slot[...] = own.astype(BF16)
        self.lines = self.go(
            [
                remote(slot, slot, self.line_sems, self.chunk * 3 + d - 1, self.me.in_line(d)[1])
                for d in range(1, 4)
            ]
        )

    def back(self):
        for copy in self.lines:
            copy.wait_recv()
        value = self.line_got[0].astype(F32)
        for d in range(1, 4):
            value = value + self.line_got[d].astype(F32)
        start = pl.multiple_of(self.mine + self.me.yz * BLOCK, BLOCK)
        block = self.total.at[pl.ds(start, BLOCK)]
        block[...] = value.astype(BF16)
        self.backs = self.go(
            [
                remote(block, block, self.back_sems, self.chunk * 15 + d - 1, self.me.in_plane(d)[1])
                for d in range(1, 16)
            ]
        )

    def twin(self):
        for copy in self.backs:
            copy.wait_recv()
        half = self.total.at[pl.ds(self.mine, HALF)]
        self.twins = self.go([remote(half, half, self.twin_sems, self.chunk, self.me.sibling())])

    def renew(self, own, probe, probe_out):
        if not own:
            self.twins[0].wait_recv()
        if probe_out is None:
            return
        part = (pl.ds(self.mine if own else self.others, HALF), slice(None))
        value = probe[part] + self.total[part].astype(F32) / (COUNT * 128)
        probe_out[part] = value

    def finish(self):
        for copy in self.sent:
            copy.wait_send()


def exchange_body(last, grad, probe_grad, tile, probe, *refs):
    if last:
        tile_out, total = refs[:2]
        refs = refs[2:]
        ext = probe_out = halo_sems = None
    else:
        tile_out, probe_out, ext = refs[:3]
        halo_sems, total, refs = refs[-2], refs[-1], refs[3:-2]
    col_out, col_got, row_out, row_got, inner = refs[:5]
    col_sems, row_sems = refs[10:12]
    me = Place()
    expected = signal_all(me, True)
    chunks = [Probe(me, i, probe_grad, total, refs[5:10], refs[12:]) for i in range(CHUNKS)]
    for chunk in chunks:
        chunk.cast()
    for plane in range(2):
        col_out[0, plane] = grad[plane, :, :H].astype(BF16)
        col_out[1, plane] = grad[plane, :, H + TC :].astype(BF16)
    wait_all(expected)
    folds = [Fold(me, 1, col_out, col_got, col_sems, plane) for plane in range(2)]
    row_folds = [Fold(me, 0, row_out, row_got, row_sems, plane) for plane in range(2)]
    halos = []
    for chunk in chunks:
        chunk.pair()
    for fold in folds:
        fold.start()
    if not last:
        for plane in range(2):
            halos.append(Halo(me, ext, halo_sems, plane))
            halos[-1].clear(ext, plane)
    for plane in range(2):
        inner[plane] = grad[plane, :, H : H + TC]
    for chunk in chunks:
        chunk.plane()

    def fold_cols(plane):
        def add(side):
            part = slice(0, H) if side == 0 else slice(TC - H, TC)
            inner[plane, :, part] += col_got[side, plane].astype(F32)

        folds[plane].arrive(add)
        row_out[0, plane] = inner[plane, :H].astype(BF16)
        row_out[1, plane] = inner[plane, H + TR :].astype(BF16)
        row_folds[plane].start()

    for plane in range(2):
        fold_cols(plane)
    power = None
    for m in range(MODES):
        for part in range(2):
            start = (m * 2 + part) * S
            value = probe[start : start + S, :].astype(BF16).astype(F32)
            power = value * value if power is None else power + value * value
    scale = 1.0 / (jnp.max(power, axis=(0, 1), keepdims=True) + EPSILON)

    def fold_rows(plane):
        def add(side):
            part = slice(H, S) if side == 0 else slice(TR, TR + H)
            inner[plane, part] += row_got[side, plane].astype(F32)

        row_folds[plane].arrive(add)
        value = inner[plane, H : H + TR] * scale
        if last:
            tile_out[plane] = value
        else:
            value = tile[plane] + value
            tile_out[plane] = value
            ext[plane, H : H + TR, H : H + TC] = value.astype(BF16)
            halos[plane].start()

    for step in ORDER:
        kind, index = step[:-1], int(step[-1])
        if kind == "rows":
            fold_rows(index)
        elif kind in ("line", "back", "twin"):
            if index < CHUNKS:
                getattr(chunks[index], kind)()
        elif kind == "own" and index < CHUNKS:
            chunks[index].renew(True, probe, probe_out)
        elif kind == "rest" and index < CHUNKS:
            chunks[index].renew(False, probe, probe_out)
    for halo in halos:
        halo.wait()
    for chunk in chunks:
        chunk.finish()
    for fold in folds + row_folds:
        fold.finish()


def exchange(last, grad, probe_grad, tile, probe):
    sizes = [((2, TR, TC), F32), ((ROWS, S), BF16 if last else F32)]
    if not last:
        sizes += [((2, ER, EC), BF16)]
    vmem = pl.BlockSpec(memory_space=pltpu.VMEM)
    dma = pltpu.SemaphoreType.DMA
    scratch = [
        pltpu.VMEM((2, 2, ER, H), BF16),
        pltpu.VMEM((2, 2, ER, H), BF16),
        pltpu.VMEM((2, 2, H, TC), BF16),
        pltpu.VMEM((2, 2, H, TC), BF16),
        pltpu.VMEM((2, ER, TC), F32),
        pltpu.VMEM((CHUNKS, HALF, S), BF16),
        pltpu.VMEM((CHUNKS, HALF, S), BF16),
        pltpu.VMEM((CHUNKS, HALF, S), BF16),
        pltpu.VMEM((CHUNKS, 15, BLOCK, S), BF16),
        pltpu.VMEM((CHUNKS, 4, BLOCK, S), BF16),
        dma((2, 4)),
        dma((2, 4)),
        dma((2, CHUNKS)),
        dma((2, 15 * CHUNKS)),
        dma((2, 3 * CHUNKS)),
        dma((2, 15 * CHUNKS)),
        dma((2, CHUNKS)),
    ]
    if not last:
        scratch += [dma((2, 16)), pltpu.VMEM((ROWS, S), BF16)]
    return pl.pallas_call(
        functools.partial(exchange_body, last),
        out_shape=[jax.ShapeDtypeStruct(*size) for size in sizes],
        in_specs=[vmem] * 4,
        out_specs=[vmem] * len(sizes),
        scratch_shapes=scratch,
        compiler_params=pltpu.CompilerParams(
            collective_id=2 if last else 1, has_side_effects=True, vmem_limit_bytes=40 * MIB
        ),
        name="last_exchange" if last else "exchange",
    )(grad, probe_grad.reshape(ROWS, S), tile, probe)


def finish_body(tile, step, probe, total, tile_out, probe_out, tile_new, probe_new, sems):
    copies = []
    for p in range(2):
        tile_new[p] = tile[p] + step[p]
        copies.append(pltpu.make_async_copy(tile_new.at[p], tile_out.at[p], sems.at[p]))
        copies[-1].start()
    for i in range(4):
        part = pl.ds(i * 512, 512)
        probe_new[part] = probe[part] + total[part].astype(F32) / (COUNT * 128)
        copies.append(
            pltpu.make_async_copy(probe_new.at[part], probe_out.at[part], sems.at[2 + i])
        )
        copies[-1].start()
    for copy in copies:
        copy.wait()


def finish(tile, step, probe, total):
    vmem, hbm = (pl.BlockSpec(memory_space=space) for space in (pltpu.VMEM, pltpu.HBM))
    return pl.pallas_call(
        finish_body,
        out_shape=[
            jax.ShapeDtypeStruct(tile.shape, F32),
            jax.ShapeDtypeStruct(probe.shape, F32),
        ],
        in_specs=[vmem] * 4,
        out_specs=[hbm] * 2,
        scratch_shapes=[
            pltpu.VMEM(tile.shape, F32),
            pltpu.VMEM(probe.shape, F32),
            pltpu.SemaphoreType.DMA((6,)),
        ],
        compiler_params=pltpu.CompilerParams(vmem_limit_bytes=16 * MIB),
        name="finish",
    )(tile, step, probe, total)


def shards(object_field, probe_modes, amplitude, offsets):
    probe = probe_modes.reshape(ROWS, S)
    tile = object_field
    ext = first_halo(tile)
    for turn in range(ITERS):
        grad, probe_grad = propagate(offsets.T, ext, probe.reshape(MODES, 2, S, S), amplitude)
        last = turn + 1 == ITERS
        results = exchange(last, grad, probe_grad, tile, probe)
        if last:
            tile, probe = finish(tile, results[0], probe, results[1])
        else:
            tile, probe, ext = results
    return tile, probe.reshape(MODES, 2, S, S)


def solution(mesh):
    split = Mesh(mesh.devices.reshape(4, 4, 4, 2), AXES)
    return jax.shard_map(
        shards,
        mesh=split,
        in_specs=(
            P(None, AXES[:2], AXES[2:]),
            P(),
            P(AXES, None, None),
            P(AXES, None),
        ),
        out_specs=(P(None, AXES[:2], AXES[2:]), P()),
        check_vma=False,
    )
```

```python
import functools

import jax
import jax.numpy as jnp
import ml_dtypes
import numpy as np
from jax import lax
from jax.experimental import pallas as pl
from jax.experimental.pallas import tpu as pltpu
from jax.sharding import Mesh
from jax.sharding import PartitionSpec as P

ITERS = 2
AXES = ("dp_0", "dp_1", "obj_0", "obj_1")
EPSILON = 1e-06
F32, BF16 = jnp.float32, jnp.bfloat16
S = 256
H = S // 2
TR, TC = 256, 512
ER, EC = TR + S, TC + S
MODES, COUNT = 4, 6
GROUP = 3
ROWS = MODES * 2 * S
CHUNKS = 2
CHUNK = ROWS // CHUNKS
HALF, BLOCK = CHUNK // 2, CHUNK // 32
ORDER = (
    "line0",
    "line1",
    "back0",
    "back1",
    "rows0",
    "rows1",
    "twin0",
    "own0",
    "twin1",
    "own1",
    "rest0",
    "rest1",
)
MIB = 1 << 20


def dft_tables():
    counter = np.arange(S)
    angle = 2.0 * np.pi * (counter[:, None] * counter[None, :] % S) / S
    re = (np.cos(angle) / 16.0).astype(np.float32).astype(ml_dtypes.bfloat16)
    im = (-np.sin(angle) / 16.0).astype(np.float32).astype(ml_dtypes.bfloat16)
    return np.block([[re, -im], [im, re]])


def propagate_body(
    offs, ext, probe_in, amp, plus, grad, probe_grad,
    ext32, probe, patches, waves, halves, fars, minus,
):
    turn = pl.program_id(0)
    me = Place()

    def by_rows(ref, value):
        @pl.loop(0, ref.shape[0] // 64)
        def _(i):
            rows = pl.ds(i * 64, 64)
            ref[rows] = value(rows)

    @pl.when(turn == 0)
    def _():
        minus[:S, :S] = plus[:S, :S]
        minus[S:, S:] = plus[S:, S:]
        minus[:S, S:] = plus[S:, :S]
        minus[S:, :S] = plus[:S, S:]
        for p in range(2):
            by_rows(grad.at[p], lambda rows: jnp.zeros((64, EC), F32))
            by_rows(ext32.at[p], lambda rows: ext[p, rows].astype(F32))
            for m in range(MODES):
                by_rows(probe_grad.at[m, p], lambda rows: jnp.zeros((64, S), F32))
                by_rows(
                    probe.at[m, p], lambda rows: probe_in[m, p, rows].astype(BF16).astype(F32)
                )

    lane = lax.broadcasted_iota(jnp.int32, (S + 8, 128), 1)

    def place(a):
        row = offs[0, turn * GROUP + a] - me.dp * TR + H
        col = offs[1, turn * GROUP + a] - me.obj * TC + H
        row_base = pl.multiple_of((row // 8) * 8, 8)
        col_block = col // 128

        def cols(i):
            return pl.ds(pl.multiple_of((col_block + i) * 128, 128), 128)

        return pl.ds(row_base, S + 8), row - row_base, cols, col - col_block * 128

    def left(table, wave, half, m):
        mid = jnp.dot(table[...], wave[m], preferred_element_type=F32).astype(BF16)
        half[m * S : (m + 1) * S, :S] = mid[:S]
        half[m * S : (m + 1) * S, S:] = mid[S:]

    def forward(a):
        patch, wave, half, far = patches.at[a], waves.at[a], halves.at[a], fars.at[a]
        rows, row_shift, cols, shift = place(a)
        for p in range(2):
            x = [
                pltpu.roll(ext32[p, rows, cols(i)], lax.rem(128 - shift, 128), 1) for i in range(3)
            ]
            for i in range(2):
                joined = jnp.where(lane < 128 - shift, x[i], x[i + 1])
                joined = pltpu.roll(joined, lax.rem(S + 8 - row_shift, S + 8), 0)
                patch[p, :, i * 128 : (i + 1) * 128] = joined[:S]
        for m in range(MODES):
            qr, qi = probe[m, 0], probe[m, 1]
            pr, pi = patch[0], patch[1]
            wave[m, :S, :] = (qr * pr - qi * pi).astype(BF16)
            wave[m, S:, :] = (qr * pi + qi * pr).astype(BF16)
            left(plus, wave, half, m)
        far[...] = jnp.dot(half[...], minus[...], preferred_element_type=F32)

    def backward(a):
        patch, wave, half, far = patches.at[a], waves.at[a], halves.at[a], fars.at[a]
        rows, row_shift, cols, shift = place(a)
        intensity = None
        for m in range(MODES):
            fr, fi = far[m * S : (m + 1) * S, :S], far[m * S : (m + 1) * S, S:]
            term = fr * fr + fi * fi
            intensity = term if intensity is None else intensity + term
        ratio = amp[a] * jnp.minimum(lax.rsqrt(intensity), 1.0) - 1.0
        for m in range(MODES):
            wave[m, :S, :] = (far[m * S : (m + 1) * S, :S] * ratio).astype(BF16)
            wave[m, S:, :] = (far[m * S : (m + 1) * S, S:] * ratio).astype(BF16)
            left(minus, wave, half, m)
        far[...] = jnp.dot(half[...], plus[...], preferred_element_type=F32)
        gr = gi = None
        for m in range(MODES):
            cr, ci = far[m * S : (m + 1) * S, :S], far[m * S : (m + 1) * S, S:]
            qr, qi = probe[m, 0], probe[m, 1]
            to_re, to_im = qr * cr + qi * ci, qr * ci - qi * cr
            gr = to_re if gr is None else gr + to_re
            gi = to_im if gi is None else gi + to_im
            pr, pi = patch[0], patch[1]
            probe_grad[m, 0] += pr * cr + pi * ci
            probe_grad[m, 1] += pr * ci - pi * cr
        for p, value in enumerate((gr, gi)):
            value = jnp.concatenate([value, jnp.zeros((8, S), F32)], 0)
            x = [
                pltpu.roll(pltpu.roll(value[:, i * 128 : (i + 1) * 128], row_shift, 0), shift, 1)
                for i in range(2)
            ]
            zero = jnp.zeros_like(x[0])
            parts = (
                jnp.where(lane >= shift, x[0], zero),
                jnp.where(lane >= shift, x[1], x[0]),
                jnp.where(lane >= shift, zero, x[1]),
            )
            for i in range(3):
                grad[p, rows, cols(i)] += parts[i]

    for a in range(GROUP):
        forward(a)
    for a in range(GROUP):
        backward(a)


def propagate(offs, ext, probe, amplitude):

    def whole(*shape):
        return pl.BlockSpec(shape, lambda n, o: (0,) * len(shape))

    return pl.pallas_call(
        propagate_body,
        grid_spec=pltpu.PrefetchScalarGridSpec(
            num_scalar_prefetch=1,
            grid=(COUNT // GROUP,),
            in_specs=[
                whole(2, ER, EC),
                whole(MODES, 2, S, S),
                pl.BlockSpec((GROUP, S, S), lambda n, o: (n, 0, 0)),
                whole(2 * S, 2 * S),
            ],
            out_specs=[whole(2, ER, EC), whole(MODES, 2, S, S)],
            scratch_shapes=[
                pltpu.VMEM((2, ER, EC), F32),
                pltpu.VMEM((MODES, 2, S, S), F32),
                pltpu.VMEM((GROUP, 2, S, S), F32),
                pltpu.VMEM((GROUP, MODES, 2 * S, S), BF16),
                pltpu.VMEM((GROUP, MODES * S, 2 * S), BF16),
                pltpu.VMEM((GROUP, MODES * S, 2 * S), F32),
                pltpu.VMEM((2 * S, 2 * S), BF16),
            ],
        ),
        out_shape=[
            jax.ShapeDtypeStruct((2, ER, EC), F32),
            jax.ShapeDtypeStruct((MODES, 2, S, S), F32),
        ],
        compiler_params=pltpu.CompilerParams(
            dimension_semantics=("arbitrary",), vmem_limit_bytes=36 * MIB
        ),
        name="propagate",
    )(offs, ext, probe, amplitude, jnp.asarray(dft_tables()))


NEAR = [(a, b) for a in (-1, 0, 1) for b in (-1, 0, 1) if (a, b) != (0, 0)]


class Place:
    def __init__(self):
        self.z, self.x, self.y, self.c = (lax.axis_index(name) for name in AXES)
        self.dp = self.z * 4 + self.x
        self.obj = self.y * 2 + self.c
        self.yz = self.y * 4 + self.z

    def has(self, a, b):
        found = None
        for step, place, count in ((a, self.dp, 16), (b, self.obj, 8)):
            if step:
                test = place > 0 if step < 0 else place < count - 1
                found = test if found is None else jnp.logical_and(found, test)
        return found

    def near(self, a, b):
        dp, obj = self.dp + a, self.obj + b
        return (dp // 4, dp % 4, obj // 2, obj % 2)

    def sibling(self):
        return (self.z, self.x, self.y, 1 - self.c)

    def in_plane(self, d):
        other = (self.yz + d) % 16
        return other, (other % 4, self.x, other // 4, self.c)

    def in_line(self, d):
        other = (self.x + d) % 4
        return other, (self.z, other, self.y, self.c)


def signal_all(me, everyone):
    barrier = pltpu.get_barrier_semaphore()
    expected = jnp.int32(0)
    for a, b in NEAR:
        there = me.has(a, b)

        @pl.when(there)
        def _():
            pl.semaphore_signal(
                barrier, inc=1, device_id=me.near(a, b), device_id_type=pl.DeviceIdType.MESH
            )

        expected = expected + there.astype(jnp.int32)
    if everyone:
        others = [me.sibling()]
        others += [me.in_plane(d)[1] for d in range(1, 16)]
        others += [me.in_line(d)[1] for d in range(1, 4)]
        for other in others:
            pl.semaphore_signal(
                barrier, inc=1, device_id=other, device_id_type=pl.DeviceIdType.MESH
            )
        expected = expected + len(others)
    return expected


def wait_all(expected):
    pl.semaphore_wait(pltpu.get_barrier_semaphore(), expected)


def remote(src, dst, sems, index, device):
    return pltpu.make_async_remote_copy(
        src_ref=src,
        dst_ref=dst,
        send_sem=sems.at[0, index],
        recv_sem=sems.at[1, index],
        device_id=device,
        device_id_type=pl.DeviceIdType.MESH,
    )


def span(step, size, sending):
    if step == 0:
        return pl.ds(H, size)
    if sending:
        return pl.ds(H if step < 0 else size, H)
    return pl.ds(0 if step < 0 else size + H, H)


class Halo:
    def __init__(self, me, ext, sems, plane):
        self.me = me
        self.copies = []
        for i, (a, b) in enumerate(NEAR):
            copy = remote(
                ext.at[plane, span(a, TR, True), span(b, TC, True)],
                ext.at[plane, span(-a, TR, False), span(-b, TC, False)],
                sems,
                plane * 8 + i,
                me.near(a, b),
            )
            self.copies.append((a, b, copy))

    def clear(self, ext, plane):
        for a, b in NEAR:

            @pl.when(jnp.logical_not(self.me.has(a, b)))
            def _():
                part = (plane, span(a, TR, False), span(b, TC, False))
                ext[part] = jnp.zeros(ext.at[part].shape, ext.dtype)

    def start(self):
        for a, b, copy in self.copies:
            pl.when(self.me.has(a, b))(copy.start)

    def wait(self):
        for a, b, copy in self.copies:
            pl.when(self.me.has(-a, -b))(copy.wait_recv)
        for a, b, copy in self.copies:
            pl.when(self.me.has(a, b))(copy.wait_send)


def halo_body(tile, ext, local, sems, local_sems):
    me = Place()
    loads = [
        pltpu.make_async_copy(tile.at[plane], local.at[plane], local_sems.at[plane])
        for plane in range(2)
    ]
    for load in loads:
        load.start()
    expected = signal_all(me, False)
    halos = [Halo(me, ext, sems, plane) for plane in range(2)]
    for plane in range(2):
        halos[plane].clear(ext, plane)
    for plane in range(2):
        loads[plane].wait()
        ext[plane, H : H + TR, H : H + TC] = local[plane].astype(BF16)
    wait_all(expected)
    for halo in halos:
        halo.start()
    for halo in halos:
        halo.wait()


def first_halo(tile):
    return pl.pallas_call(
        halo_body,
        out_shape=jax.ShapeDtypeStruct((2, ER, EC), BF16),
        in_specs=[pl.BlockSpec(memory_space=pltpu.HBM)],
        out_specs=pl.BlockSpec(memory_space=pltpu.VMEM),
        scratch_shapes=[
            pltpu.VMEM((2, TR, TC), F32),
            pltpu.SemaphoreType.DMA((2, 16)),
            pltpu.SemaphoreType.DMA((2,)),
        ],
        cost_estimate=pl.CostEstimate(flops=10**10, bytes_accessed=10**6, transcendentals=0),
        compiler_params=pltpu.CompilerParams(
            collective_id=0, has_side_effects=True, vmem_limit_bytes=16 * MIB
        ),
        name="first_halo",
    )(tile)


class Fold:
    def __init__(self, me, axis, out, got, sems, plane):
        self.me, self.axis = me, axis
        self.copies = []
        for side, step in enumerate((-1, 1)):
            at = (step, 0) if axis == 0 else (0, step)
            copy = remote(
                out.at[side, plane], got.at[1 - side, plane], sems, plane * 2 + side, me.near(*at)
            )
            self.copies.append((step, at, copy))

    def start(self):
        for step, at, copy in self.copies:
            pl.when(self.me.has(*at))(copy.start)

    def arrive(self, add):
        for side, (step, at, copy) in enumerate(self.copies):
            back = (-at[0], -at[1])

            @pl.when(self.me.has(*back))
            def _():
                copy.wait_recv()
                add(1 - side)

    def finish(self):
        for step, at, copy in self.copies:
            pl.when(self.me.has(*at))(copy.wait_send)


class Probe:
    def __init__(self, me, chunk, probe_grad, total, bufs, sems):
        self.me, self.chunk, self.source, self.total = me, chunk, probe_grad, total
        self.pair_out, self.pair_got, self.plane_out, self.plane_got, self.line_got = (
            buf.at[chunk] for buf in bufs
        )
        self.pair_sems, self.plane_sems, self.line_sems, self.back_sems, self.twin_sems = sems
        start = chunk * CHUNK
        self.mine = pl.multiple_of(start + me.c * HALF, HALF)
        self.others = pl.multiple_of(start + (1 - me.c) * HALF, HALF)
        self.sent = []

    def go(self, copies):
        for copy in copies:
            copy.start()
        self.sent += copies
        return copies

    def cast(self):
        self.pair_out[...] = self.source[pl.ds(self.others, HALF), :].astype(BF16)

    def pair(self):
        self.pairs = self.go(
            [remote(self.pair_out, self.pair_got, self.pair_sems, self.chunk, self.me.sibling())]
        )

    def plane(self):
        self.pairs[0].wait_recv()
        own = self.source[pl.ds(self.mine, HALF), :]
        self.plane_out[...] = (own + self.pair_got[...].astype(F32)).astype(BF16)
        copies = []
        for d in range(1, 16):
            other, device = self.me.in_plane(d)
            copies.append(
                remote(
                    self.plane_out.at[pl.ds(pl.multiple_of(other * BLOCK, BLOCK), BLOCK)],
                    self.plane_got.at[d - 1],
                    self.plane_sems,
                    self.chunk * 15 + d - 1,
                    device,
                )
            )
        self.planes = self.go(copies)

    def line(self):
        for copy in self.planes:
            copy.wait_recv()
        own = self.plane_out[pl.ds(pl.multiple_of(self.me.yz * BLOCK, BLOCK), BLOCK), :].astype(F32)
        for d in range(15):
            own = own + self.plane_got[d].astype(F32)
        slot = self.line_got.at[self.me.x]
        slot[...] = own.astype(BF16)
        self.lines = self.go(
            [
                remote(slot, slot, self.line_sems, self.chunk * 3 + d - 1, self.me.in_line(d)[1])
                for d in range(1, 4)
            ]
        )

    def back(self):
        for copy in self.lines:
            copy.wait_recv()
        value = self.line_got[0].astype(F32)
        for d in range(1, 4):
            value = value + self.line_got[d].astype(F32)
        start = pl.multiple_of(self.mine + self.me.yz * BLOCK, BLOCK)
        block = self.total.at[pl.ds(start, BLOCK)]
        block[...] = value.astype(BF16)
        self.backs = self.go(
            [
                remote(block, block, self.back_sems, self.chunk * 15 + d - 1, self.me.in_plane(d)[1])
                for d in range(1, 16)
            ]
        )

    def twin(self):
        for copy in self.backs:
            copy.wait_recv()
        half = self.total.at[pl.ds(self.mine, HALF)]
        self.twins = self.go([remote(half, half, self.twin_sems, self.chunk, self.me.sibling())])

    def renew(self, own, probe, probe_out):
        if not own:
            self.twins[0].wait_recv()
        if probe_out is None:
            return
        part = (pl.ds(self.mine if own else self.others, HALF), slice(None))
        value = probe[part] + self.total[part].astype(F32) / (COUNT * 128)
        probe_out[part] = value

    def finish(self):
        for copy in self.sent:
            copy.wait_send()


def exchange_body(last, grad, probe_grad, tile, probe, *refs):
    if last:
        tile_out, total = refs[:2]
        refs = refs[2:]
        ext = probe_out = halo_sems = None
    else:
        tile_out, probe_out, ext = refs[:3]
        halo_sems, total, refs = refs[-2], refs[-1], refs[3:-2]
    col_out, col_got, row_out, row_got, inner = refs[:5]
    col_sems, row_sems = refs[10:12]
    me = Place()
    expected = signal_all(me, True)
    chunks = [Probe(me, i, probe_grad, total, refs[5:10], refs[12:]) for i in range(CHUNKS)]
    for chunk in chunks:
        chunk.cast()
    for plane in range(2):
        col_out[0, plane] = grad[plane, :, :H].astype(BF16)
        col_out[1, plane] = grad[plane, :, H + TC :].astype(BF16)
    wait_all(expected)
    folds = [Fold(me, 1, col_out, col_got, col_sems, plane) for plane in range(2)]
    row_folds = [Fold(me, 0, row_out, row_got, row_sems, plane) for plane in range(2)]
    halos = []
    for chunk in chunks:
        chunk.pair()
    for fold in folds:
        fold.start()
    if not last:
        for plane in range(2):
            halos.append(Halo(me, ext, halo_sems, plane))
            halos[-1].clear(ext, plane)
    for plane in range(2):
        inner[plane] = grad[plane, :, H : H + TC]
    for chunk in chunks:
        chunk.plane()

    def fold_cols(plane):
        def add(side):
            part = slice(0, H) if side == 0 else slice(TC - H, TC)
            inner[plane, :, part] += col_got[side, plane].astype(F32)

        folds[plane].arrive(add)
        row_out[0, plane] = inner[plane, :H].astype(BF16)
        row_out[1, plane] = inner[plane, H + TR :].astype(BF16)
        row_folds[plane].start()

    for plane in range(2):
        fold_cols(plane)
    power = None
    for m in range(MODES):
        for part in range(2):
            start = (m * 2 + part) * S
            value = probe[start : start + S, :].astype(BF16).astype(F32)
            power = value * value if power is None else power + value * value
    scale = 1.0 / (jnp.max(power, axis=(0, 1), keepdims=True) + EPSILON)

    def fold_rows(plane):
        def add(side):
            part = slice(H, S) if side == 0 else slice(TR, TR + H)
            inner[plane, part] += row_got[side, plane].astype(F32)

        row_folds[plane].arrive(add)
        value = inner[plane, H : H + TR] * scale
        if last:
            tile_out[plane] = value
        else:
            value = tile[plane] + value
            tile_out[plane] = value
            ext[plane, H : H + TR, H : H + TC] = value.astype(BF16)
            halos[plane].start()

    for step in ORDER:
        kind, index = step[:-1], int(step[-1])
        if kind == "rows":
            fold_rows(index)
        elif kind in ("line", "back", "twin"):
            if index < CHUNKS:
                getattr(chunks[index], kind)()
        elif kind == "own" and index < CHUNKS:
            chunks[index].renew(True, probe, probe_out)
        elif kind == "rest" and index < CHUNKS:
            chunks[index].renew(False, probe, probe_out)
    for halo in halos:
        halo.wait()
    for chunk in chunks:
        chunk.finish()
    for fold in folds + row_folds:
        fold.finish()


def exchange(last, grad, probe_grad, tile, probe):
    sizes = [((2, TR, TC), F32), ((ROWS, S), BF16 if last else F32)]
    if not last:
        sizes += [((2, ER, EC), BF16)]
    vmem = pl.BlockSpec(memory_space=pltpu.VMEM)
    dma = pltpu.SemaphoreType.DMA
    scratch = [
        pltpu.VMEM((2, 2, ER, H), BF16),
        pltpu.VMEM((2, 2, ER, H), BF16),
        pltpu.VMEM((2, 2, H, TC), BF16),
        pltpu.VMEM((2, 2, H, TC), BF16),
        pltpu.VMEM((2, ER, TC), F32),
        pltpu.VMEM((CHUNKS, HALF, S), BF16),
        pltpu.VMEM((CHUNKS, HALF, S), BF16),
        pltpu.VMEM((CHUNKS, HALF, S), BF16),
        pltpu.VMEM((CHUNKS, 15, BLOCK, S), BF16),
        pltpu.VMEM((CHUNKS, 4, BLOCK, S), BF16),
        dma((2, 4)),
        dma((2, 4)),
        dma((2, CHUNKS)),
        dma((2, 15 * CHUNKS)),
        dma((2, 3 * CHUNKS)),
        dma((2, 15 * CHUNKS)),
        dma((2, CHUNKS)),
    ]
    if not last:
        scratch += [dma((2, 16)), pltpu.VMEM((ROWS, S), BF16)]
    return pl.pallas_call(
        functools.partial(exchange_body, last),
        out_shape=[jax.ShapeDtypeStruct(*size) for size in sizes],
        in_specs=[vmem] * 4,
        out_specs=[vmem] * len(sizes),
        scratch_shapes=scratch,
        compiler_params=pltpu.CompilerParams(
            collective_id=2 if last else 1, has_side_effects=True, vmem_limit_bytes=40 * MIB
        ),
        name="last_exchange" if last else "exchange",
    )(grad, probe_grad.reshape(ROWS, S), tile, probe)


def finish_body(tile, step, probe, total, tile_out, probe_out, tile_new, probe_new, sems):
    copies = []
    for p in range(2):
        tile_new[p] = tile[p] + step[p]
        copies.append(pltpu.make_async_copy(tile_new.at[p], tile_out.at[p], sems.at[p]))
        copies[-1].start()
    for i in range(4):
        part = pl.ds(i * 512, 512)
        probe_new[part] = probe[part] + total[part].astype(F32) / (COUNT * 128)
        copies.append(
            pltpu.make_async_copy(probe_new.at[part], probe_out.at[part], sems.at[2 + i])
        )
        copies[-1].start()
    for copy in copies:
        copy.wait()


def finish(tile, step, probe, total):
    vmem, hbm = (pl.BlockSpec(memory_space=space) for space in (pltpu.VMEM, pltpu.HBM))
    return pl.pallas_call(
        finish_body,
        out_shape=[
            jax.ShapeDtypeStruct(tile.shape, F32),
            jax.ShapeDtypeStruct(probe.shape, F32),
        ],
        in_specs=[vmem] * 4,
        out_specs=[hbm] * 2,
        scratch_shapes=[
            pltpu.VMEM(tile.shape, F32),
            pltpu.VMEM(probe.shape, F32),
            pltpu.SemaphoreType.DMA((6,)),
        ],
        compiler_params=pltpu.CompilerParams(vmem_limit_bytes=16 * MIB),
        name="finish",
    )(tile, step, probe, total)


def shards(object_field, probe_modes, amplitude, offsets):
    probe = probe_modes.reshape(ROWS, S)
    tile = object_field
    ext = first_halo(tile)
    for turn in range(ITERS):
        grad, probe_grad = propagate(offsets.T, ext, probe.reshape(MODES, 2, S, S), amplitude)
        last = turn + 1 == ITERS
        results = exchange(last, grad, probe_grad, tile, probe)
        if last:
            tile, probe = finish(tile, results[0], probe, results[1])
        else:
            tile, probe, ext = results
    return tile, probe.reshape(MODES, 2, S, S)


def solution(mesh):
    split = Mesh(mesh.devices.reshape(4, 4, 4, 2), AXES)
    return jax.shard_map(
        shards,
        mesh=split,
        in_specs=(
            P(None, AXES[:2], AXES[2:]),
            P(),
            P(AXES, None, None),
            P(AXES, None),
        ),
        out_specs=(P(None, AXES[:2], AXES[2:]), P()),
        check_vma=False,
    )
```

```python
import functools

import jax
import jax.numpy as jnp
import ml_dtypes
import numpy as np
from jax import lax
from jax.experimental import pallas as pl
from jax.experimental.pallas import tpu as pltpu
from jax.sharding import Mesh
from jax.sharding import PartitionSpec as P

ITERS = 2
AXES = ("dp_0", "dp_1", "obj_0", "obj_1")
EPSILON = 1e-06
F32, BF16 = jnp.float32, jnp.bfloat16
S = 256
H = S // 2
TR, TC = 256, 512
ER, EC = TR + S, TC + S
MODES, COUNT = 4, 6
GROUP = 3
ROWS = MODES * 2 * S
CHUNKS = 2
CHUNK = ROWS // CHUNKS
HALF, BLOCK = CHUNK // 2, CHUNK // 32
ORDER = (
    "line0",
    "line1",
    "back0",
    "back1",
    "rows0",
    "rows1",
    "twin0",
    "own0",
    "twin1",
    "own1",
    "rest0",
    "rest1",
)
MIB = 1 << 20


def dft_tables():
    counter = np.arange(S)
    angle = 2.0 * np.pi * (counter[:, None] * counter[None, :] % S) / S
    re = (np.cos(angle) / 16.0).astype(np.float32).astype(ml_dtypes.bfloat16)
    im = (-np.sin(angle) / 16.0).astype(np.float32).astype(ml_dtypes.bfloat16)
    return np.block([[re, -im], [im, re]])


def propagate_body(
    offs, ext, probe_in, amp, plus, grad, probe_grad,
    ext32, probe, patches, waves, halves, fars, minus,
):
    turn = pl.program_id(0)
    me = Place()

    def by_rows(ref, value):
        @pl.loop(0, ref.shape[0] // 64)
        def _(i):
            rows = pl.ds(i * 64, 64)
            ref[rows] = value(rows)

    @pl.when(turn == 0)
    def _():
        minus[:S, :S] = plus[:S, :S]
        minus[S:, S:] = plus[S:, S:]
        minus[:S, S:] = plus[S:, :S]
        minus[S:, :S] = plus[:S, S:]
        for p in range(2):
            by_rows(grad.at[p], lambda rows: jnp.zeros((64, EC), F32))
            by_rows(ext32.at[p], lambda rows: ext[p, rows].astype(F32))
            for m in range(MODES):
                by_rows(probe_grad.at[m, p], lambda rows: jnp.zeros((64, S), F32))
                by_rows(
                    probe.at[m, p], lambda rows: probe_in[m, p, rows].astype(BF16).astype(F32)
                )

    lane = lax.broadcasted_iota(jnp.int32, (S + 8, 128), 1)

    def place(a):
        row = offs[0, turn * GROUP + a] - me.dp * TR + H
        col = offs[1, turn * GROUP + a] - me.obj * TC + H
        row_base = pl.multiple_of((row // 8) * 8, 8)
        col_block = col // 128

        def cols(i):
            return pl.ds(pl.multiple_of((col_block + i) * 128, 128), 128)

        return pl.ds(row_base, S + 8), row - row_base, cols, col - col_block * 128

    def left(table, wave, half, m):
        mid = jnp.dot(table[...], wave[m], preferred_element_type=F32).astype(BF16)
        half[m * S : (m + 1) * S, :S] = mid[:S]
        half[m * S : (m + 1) * S, S:] = mid[S:]

    def forward(a):
        patch, wave, half, far = patches.at[a], waves.at[a], halves.at[a], fars.at[a]
        rows, row_shift, cols, shift = place(a)
        for p in range(2):
            x = [
                pltpu.roll(ext32[p, rows, cols(i)], lax.rem(128 - shift, 128), 1) for i in range(3)
            ]
            for i in range(2):
                joined = jnp.where(lane < 128 - shift, x[i], x[i + 1])
                joined = pltpu.roll(joined, lax.rem(S + 8 - row_shift, S + 8), 0)
                patch[p, :, i * 128 : (i + 1) * 128] = joined[:S]
        for m in range(MODES):
            qr, qi = probe[m, 0], probe[m, 1]
            pr, pi = patch[0], patch[1]
            wave[m, :S, :] = (qr * pr - qi * pi).astype(BF16)
            wave[m, S:, :] = (qr * pi + qi * pr).astype(BF16)
            left(plus, wave, half, m)
        far[...] = jnp.dot(half[...], minus[...], preferred_element_type=F32)

    def backward(a):
        patch, wave, half, far = patches.at[a], waves.at[a], halves.at[a], fars.at[a]
        rows, row_shift, cols, shift = place(a)
        intensity = None
        for m in range(MODES):
            fr, fi = far[m * S : (m + 1) * S, :S], far[m * S : (m + 1) * S, S:]
            term = fr * fr + fi * fi
            intensity = term if intensity is None else intensity + term
        ratio = amp[a] * jnp.minimum(lax.rsqrt(intensity), 1.0) - 1.0
        for m in range(MODES):
            wave[m, :S, :] = (far[m * S : (m + 1) * S, :S] * ratio).astype(BF16)
            wave[m, S:, :] = (far[m * S : (m + 1) * S, S:] * ratio).astype(BF16)
            left(minus, wave, half, m)
        far[...] = jnp.dot(half[...], plus[...], preferred_element_type=F32)
        gr = gi = None
        for m in range(MODES):
            cr, ci = far[m * S : (m + 1) * S, :S], far[m * S : (m + 1) * S, S:]
            qr, qi = probe[m, 0], probe[m, 1]
            to_re, to_im = qr * cr + qi * ci, qr * ci - qi * cr
            gr = to_re if gr is None else gr + to_re
            gi = to_im if gi is None else gi + to_im
            pr, pi = patch[0], patch[1]
            probe_grad[m, 0] += pr * cr + pi * ci
            probe_grad[m, 1] += pr * ci - pi * cr
        for p, value in enumerate((gr, gi)):
            value = jnp.concatenate([value, jnp.zeros((8, S), F32)], 0)
            x = [
                pltpu.roll(pltpu.roll(value[:, i * 128 : (i + 1) * 128], row_shift, 0), shift, 1)
                for i in range(2)
            ]
            zero = jnp.zeros_like(x[0])
            parts = (
                jnp.where(lane >= shift, x[0], zero),
                jnp.where(lane >= shift, x[1], x[0]),
                jnp.where(lane >= shift, zero, x[1]),
            )
            for i in range(3):
                grad[p, rows, cols(i)] += parts[i]

    for a in range(GROUP):
        forward(a)
    for a in range(GROUP):
        backward(a)


def propagate(offs, ext, probe, amplitude):

    def whole(*shape):
        return pl.BlockSpec(shape, lambda n, o: (0,) * len(shape))

    return pl.pallas_call(
        propagate_body,
        grid_spec=pltpu.PrefetchScalarGridSpec(
            num_scalar_prefetch=1,
            grid=(COUNT // GROUP,),
            in_specs=[
                whole(2, ER, EC),
                whole(MODES, 2, S, S),
                pl.BlockSpec((GROUP, S, S), lambda n, o: (n, 0, 0)),
                whole(2 * S, 2 * S),
            ],
            out_specs=[whole(2, ER, EC), whole(MODES, 2, S, S)],
            scratch_shapes=[
                pltpu.VMEM((2, ER, EC), F32),
                pltpu.VMEM((MODES, 2, S, S), F32),
                pltpu.VMEM((GROUP, 2, S, S), F32),
                pltpu.VMEM((GROUP, MODES, 2 * S, S), BF16),
                pltpu.VMEM((GROUP, MODES * S, 2 * S), BF16),
                pltpu.VMEM((GROUP, MODES * S, 2 * S), F32),
                pltpu.VMEM((2 * S, 2 * S), BF16),
            ],
        ),
        out_shape=[
            jax.ShapeDtypeStruct((2, ER, EC), F32),
            jax.ShapeDtypeStruct((MODES, 2, S, S), F32),
        ],
        compiler_params=pltpu.CompilerParams(
            dimension_semantics=("arbitrary",), vmem_limit_bytes=36 * MIB
        ),
        name="propagate",
    )(offs, ext, probe, amplitude, jnp.asarray(dft_tables()))


NEAR = [(-1, 0), (1, 0), (-1, -1), (-1, 1), (1, -1), (1, 1), (0, -1), (0, 1)]


class Place:
    def __init__(self):
        self.z, self.x, self.y, self.c = (lax.axis_index(name) for name in AXES)
        self.dp = self.z * 4 + self.x
        self.obj = self.y * 2 + self.c
        self.yz = self.y * 4 + self.z

    def has(self, a, b):
        found = None
        for step, place, count in ((a, self.dp, 16), (b, self.obj, 8)):
            if step:
                test = place > 0 if step < 0 else place < count - 1
                found = test if found is None else jnp.logical_and(found, test)
        return found

    def near(self, a, b):
        dp, obj = self.dp + a, self.obj + b
        return (dp // 4, dp % 4, obj // 2, obj % 2)

    def sibling(self):
        return (self.z, self.x, self.y, 1 - self.c)

    def in_plane(self, d):
        other = (self.yz + d) % 16
        return other, (other % 4, self.x, other // 4, self.c)

    def in_line(self, d):
        other = (self.x + d) % 4
        return other, (self.z, other, self.y, self.c)


def signal_all(me, everyone):
    barrier = pltpu.get_barrier_semaphore()
    expected = jnp.int32(0)
    for a, b in NEAR:
        there = me.has(a, b)

        @pl.when(there)
        def _():
            pl.semaphore_signal(
                barrier, inc=1, device_id=me.near(a, b), device_id_type=pl.DeviceIdType.MESH
            )

        expected = expected + there.astype(jnp.int32)
    if everyone:
        others = [me.sibling()]
        others += [me.in_plane(d)[1] for d in range(1, 16)]
        others += [me.in_line(d)[1] for d in range(1, 4)]
        for other in others:
            pl.semaphore_signal(
                barrier, inc=1, device_id=other, device_id_type=pl.DeviceIdType.MESH
            )
        expected = expected + len(others)
    return expected


def wait_all(expected):
    pl.semaphore_wait(pltpu.get_barrier_semaphore(), expected)


def remote(src, dst, sems, index, device):
    return pltpu.make_async_remote_copy(
        src_ref=src,
        dst_ref=dst,
        send_sem=sems.at[0, index],
        recv_sem=sems.at[1, index],
        device_id=device,
        device_id_type=pl.DeviceIdType.MESH,
    )


def span(step, size, sending):
    if step == 0:
        return pl.ds(H, size)
    if sending:
        return pl.ds(H if step < 0 else size, H)
    return pl.ds(0 if step < 0 else size + H, H)


class Halo:
    def __init__(self, me, ext, sems, plane):
        self.me = me
        self.copies = []
        for i, (a, b) in enumerate(NEAR):
            copy = remote(
                ext.at[plane, span(a, TR, True), span(b, TC, True)],
                ext.at[plane, span(-a, TR, False), span(-b, TC, False)],
                sems,
                plane * 8 + i,
                me.near(a, b),
            )
            self.copies.append((a, b, copy))

    def clear(self, ext, plane):
        for a, b in NEAR:

            @pl.when(jnp.logical_not(self.me.has(a, b)))
            def _():
                part = (plane, span(a, TR, False), span(b, TC, False))
                ext[part] = jnp.zeros(ext.at[part].shape, ext.dtype)

    def start(self):
        for a, b, copy in self.copies:
            pl.when(self.me.has(a, b))(copy.start)

    def wait(self):
        for a, b, copy in self.copies:
            pl.when(self.me.has(-a, -b))(copy.wait_recv)
        for a, b, copy in self.copies:
            pl.when(self.me.has(a, b))(copy.wait_send)


def halo_body(tile, ext, sems):
    me = Place()
    expected = signal_all(me, False)
    halos = [Halo(me, ext, sems, plane) for plane in range(2)]
    for plane in range(2):
        halos[plane].clear(ext, plane)
    for plane in range(2):
        ext[plane, H : H + TR, H : H + TC] = tile[plane].astype(BF16)
    wait_all(expected)
    for halo in halos:
        halo.start()
    for halo in halos:
        halo.wait()


def first_halo(tile):
    return pl.pallas_call(
        halo_body,
        out_shape=jax.ShapeDtypeStruct((2, ER, EC), BF16),
        in_specs=[pl.BlockSpec(memory_space=pltpu.VMEM)],
        out_specs=pl.BlockSpec(memory_space=pltpu.VMEM),
        scratch_shapes=[pltpu.SemaphoreType.DMA((2, 16))],
        cost_estimate=pl.CostEstimate(flops=10**10, bytes_accessed=10**6, transcendentals=0),
        compiler_params=pltpu.CompilerParams(
            collective_id=0, has_side_effects=True, vmem_limit_bytes=16 * MIB
        ),
        name="first_halo",
    )(tile)


class Fold:
    def __init__(self, me, axis, out, got, sems, plane):
        self.me, self.axis = me, axis
        self.copies = []
        for side, step in enumerate((-1, 1)):
            at = (step, 0) if axis == 0 else (0, step)
            copy = remote(
                out.at[side, plane], got.at[1 - side, plane], sems, plane * 2 + side, me.near(*at)
            )
            self.copies.append((step, at, copy))

    def start(self):
        for step, at, copy in self.copies:
            pl.when(self.me.has(*at))(copy.start)

    def arrive(self, add):
        for side, (step, at, copy) in enumerate(self.copies):
            back = (-at[0], -at[1])

            @pl.when(self.me.has(*back))
            def _():
                copy.wait_recv()
                add(1 - side)

    def finish(self):
        for step, at, copy in self.copies:
            pl.when(self.me.has(*at))(copy.wait_send)


class Probe:
    def __init__(self, me, chunk, probe_grad, total, bufs, sems):
        self.me, self.chunk, self.source, self.total = me, chunk, probe_grad, total
        self.pair_out, self.pair_got, self.plane_out, self.plane_got, self.line_got = (
            buf.at[chunk] for buf in bufs
        )
        self.pair_sems, self.plane_sems, self.line_sems, self.back_sems, self.twin_sems = sems
        start = chunk * CHUNK
        self.mine = pl.multiple_of(start + me.c * HALF, HALF)
        self.others = pl.multiple_of(start + (1 - me.c) * HALF, HALF)
        self.sent = []

    def go(self, copies):
        for copy in copies:
            copy.start()
        self.sent += copies
        return copies

    def cast(self):
        self.pair_out[...] = self.source[pl.ds(self.others, HALF), :].astype(BF16)

    def pair(self):
        self.pairs = self.go(
            [remote(self.pair_out, self.pair_got, self.pair_sems, self.chunk, self.me.sibling())]
        )

    def plane(self):
        self.pairs[0].wait_recv()
        own = self.source[pl.ds(self.mine, HALF), :]
        self.plane_out[...] = (own + self.pair_got[...].astype(F32)).astype(BF16)
        copies = []
        for d in range(1, 16):
            other, device = self.me.in_plane(d)
            copies.append(
                remote(
                    self.plane_out.at[pl.ds(pl.multiple_of(other * BLOCK, BLOCK), BLOCK)],
                    self.plane_got.at[d - 1],
                    self.plane_sems,
                    self.chunk * 15 + d - 1,
                    device,
                )
            )
        self.planes = self.go(copies)

    def line(self):
        for copy in self.planes:
            copy.wait_recv()
        own = self.plane_out[pl.ds(pl.multiple_of(self.me.yz * BLOCK, BLOCK), BLOCK), :].astype(F32)
        for d in range(15):
            own = own + self.plane_got[d].astype(F32)
        slot = self.line_got.at[self.me.x]
        slot[...] = own.astype(BF16)
        self.lines = self.go(
            [
                remote(slot, slot, self.line_sems, self.chunk * 3 + d - 1, self.me.in_line(d)[1])
                for d in range(1, 4)
            ]
        )

    def back(self):
        for copy in self.lines:
            copy.wait_recv()
        value = self.line_got[0].astype(F32)
        for d in range(1, 4):
            value = value + self.line_got[d].astype(F32)
        start = pl.multiple_of(self.mine + self.me.yz * BLOCK, BLOCK)
        block = self.total.at[pl.ds(start, BLOCK)]
        block[...] = value.astype(BF16)
        self.backs = self.go(
            [
                remote(block, block, self.back_sems, self.chunk * 15 + d - 1, self.me.in_plane(d)[1])
                for d in range(1, 16)
            ]
        )

    def twin(self):
        for copy in self.backs:
            copy.wait_recv()
        half = self.total.at[pl.ds(self.mine, HALF)]
        self.twins = self.go([remote(half, half, self.twin_sems, self.chunk, self.me.sibling())])

    def renew(self, own, probe, probe_out):
        if not own:
            self.twins[0].wait_recv()
        if probe_out is None:
            return
        part = (pl.ds(self.mine if own else self.others, HALF), slice(None))
        value = probe[part] + self.total[part].astype(F32) / (COUNT * 128)
        probe_out[part] = value

    def finish(self):
        for copy in self.sent:
            copy.wait_send()


def exchange_body(last, grad, probe_grad, tile, probe, *refs):
    if last:
        tile_out, total = refs[:2]
        refs = refs[2:]
        ext = probe_out = halo_sems = None
    else:
        tile_out, probe_out, ext = refs[:3]
        halo_sems, total, refs = refs[-2], refs[-1], refs[3:-2]
    col_out, col_got, row_out, row_got, inner = refs[:5]
    col_sems, row_sems = refs[10:12]
    me = Place()
    expected = signal_all(me, True)
    chunks = [Probe(me, i, probe_grad, total, refs[5:10], refs[12:]) for i in range(CHUNKS)]
    for chunk in chunks:
        chunk.cast()
    for plane in range(2):
        col_out[0, plane] = grad[plane, :, :H].astype(BF16)
        col_out[1, plane] = grad[plane, :, H + TC :].astype(BF16)
    wait_all(expected)
    folds = [Fold(me, 1, col_out, col_got, col_sems, plane) for plane in range(2)]
    row_folds = [Fold(me, 0, row_out, row_got, row_sems, plane) for plane in range(2)]
    halos = []
    for chunk in chunks:
        chunk.pair()
    for fold in folds:
        fold.start()
    if not last:
        for plane in range(2):
            halos.append(Halo(me, ext, halo_sems, plane))
            halos[-1].clear(ext, plane)
    for plane in range(2):
        inner[plane] = grad[plane, :, H : H + TC]
    for chunk in chunks:
        chunk.plane()

    def fold_cols(plane):
        def add(side):
            part = slice(0, H) if side == 0 else slice(TC - H, TC)
            inner[plane, :, part] += col_got[side, plane].astype(F32)

        folds[plane].arrive(add)
        row_out[0, plane] = inner[plane, :H].astype(BF16)
        row_out[1, plane] = inner[plane, H + TR :].astype(BF16)
        row_folds[plane].start()

    for plane in range(2):
        fold_cols(plane)
    power = None
    for m in range(MODES):
        for part in range(2):
            start = (m * 2 + part) * S
            value = probe[start : start + S, :].astype(BF16).astype(F32)
            power = value * value if power is None else power + value * value
    scale = 1.0 / (jnp.max(power, axis=(0, 1), keepdims=True) + EPSILON)

    def fold_rows(plane):
        def add(side):
            part = slice(H, S) if side == 0 else slice(TR, TR + H)
            inner[plane, part] += row_got[side, plane].astype(F32)

        row_folds[plane].arrive(add)
        value = inner[plane, H : H + TR] * scale
        if last:
            tile_out[plane] = value
        else:
            value = tile[plane] + value
            tile_out[plane] = value
            ext[plane, H : H + TR, H : H + TC] = value.astype(BF16)
            halos[plane].start()

    for step in ORDER:
        kind, index = step[:-1], int(step[-1])
        if kind == "rows":
            fold_rows(index)
        elif kind in ("line", "back", "twin"):
            if index < CHUNKS:
                getattr(chunks[index], kind)()
        elif kind == "own" and index < CHUNKS:
            chunks[index].renew(True, probe, probe_out)
        elif kind == "rest" and index < CHUNKS:
            chunks[index].renew(False, probe, probe_out)
    for halo in halos:
        halo.wait()
    for chunk in chunks:
        chunk.finish()
    for fold in folds + row_folds:
        fold.finish()


def exchange(last, grad, probe_grad, tile, probe):
    sizes = [((2, TR, TC), F32), ((ROWS, S), BF16 if last else F32)]
    if not last:
        sizes += [((2, ER, EC), BF16)]
    vmem = pl.BlockSpec(memory_space=pltpu.VMEM)
    dma = pltpu.SemaphoreType.DMA
    scratch = [
        pltpu.VMEM((2, 2, ER, H), BF16),
        pltpu.VMEM((2, 2, ER, H), BF16),
        pltpu.VMEM((2, 2, H, TC), BF16),
        pltpu.VMEM((2, 2, H, TC), BF16),
        pltpu.VMEM((2, ER, TC), F32),
        pltpu.VMEM((CHUNKS, HALF, S), BF16),
        pltpu.VMEM((CHUNKS, HALF, S), BF16),
        pltpu.VMEM((CHUNKS, HALF, S), BF16),
        pltpu.VMEM((CHUNKS, 15, BLOCK, S), BF16),
        pltpu.VMEM((CHUNKS, 4, BLOCK, S), BF16),
        dma((2, 4)),
        dma((2, 4)),
        dma((2, CHUNKS)),
        dma((2, 15 * CHUNKS)),
        dma((2, 3 * CHUNKS)),
        dma((2, 15 * CHUNKS)),
        dma((2, CHUNKS)),
    ]
    if not last:
        scratch += [dma((2, 16)), pltpu.VMEM((ROWS, S), BF16)]
    return pl.pallas_call(
        functools.partial(exchange_body, last),
        out_shape=[jax.ShapeDtypeStruct(*size) for size in sizes],
        in_specs=[vmem] * 4,
        out_specs=[vmem] * len(sizes),
        scratch_shapes=scratch,
        compiler_params=pltpu.CompilerParams(
            collective_id=2 if last else 1, has_side_effects=True, vmem_limit_bytes=40 * MIB
        ),
        name="last_exchange" if last else "exchange",
    )(grad, probe_grad.reshape(ROWS, S), tile, probe)


def finish_body(tile, step, probe, total, tile_out, probe_out, tile_new, probe_new, sems):
    copies = []
    for p in range(2):
        tile_new[p] = tile[p] + step[p]
        copies.append(pltpu.make_async_copy(tile_new.at[p], tile_out.at[p], sems.at[p]))
        copies[-1].start()
    for i in range(4):
        part = pl.ds(i * 512, 512)
        probe_new[part] = probe[part] + total[part].astype(F32) / (COUNT * 128)
        copies.append(
            pltpu.make_async_copy(probe_new.at[part], probe_out.at[part], sems.at[2 + i])
        )
        copies[-1].start()
    for copy in copies:
        copy.wait()


def finish(tile, step, probe, total):
    vmem, hbm = (pl.BlockSpec(memory_space=space) for space in (pltpu.VMEM, pltpu.HBM))
    return pl.pallas_call(
        finish_body,
        out_shape=[
            jax.ShapeDtypeStruct(tile.shape, F32),
            jax.ShapeDtypeStruct(probe.shape, F32),
        ],
        in_specs=[vmem] * 4,
        out_specs=[hbm] * 2,
        scratch_shapes=[
            pltpu.VMEM(tile.shape, F32),
            pltpu.VMEM(probe.shape, F32),
            pltpu.SemaphoreType.DMA((6,)),
        ],
        compiler_params=pltpu.CompilerParams(vmem_limit_bytes=16 * MIB),
        name="finish",
    )(tile, step, probe, total)


def shards(object_field, probe_modes, amplitude, offsets):
    probe = probe_modes.reshape(ROWS, S)
    tile = object_field
    ext = first_halo(tile)
    for turn in range(ITERS):
        grad, probe_grad = propagate(offsets.T, ext, probe.reshape(MODES, 2, S, S), amplitude)
        last = turn + 1 == ITERS
        results = exchange(last, grad, probe_grad, tile, probe)
        if last:
            tile, probe = finish(tile, results[0], probe, results[1])
        else:
            tile, probe, ext = results
    return tile, probe.reshape(MODES, 2, S, S)


def solution(mesh):
    split = Mesh(mesh.devices.reshape(4, 4, 4, 2), AXES)
    return jax.shard_map(
        shards,
        mesh=split,
        in_specs=(
            P(None, AXES[:2], AXES[2:]),
            P(),
            P(AXES, None, None),
            P(AXES, None),
        ),
        out_specs=(P(None, AXES[:2], AXES[2:]), P()),
        check_vma=False,
    )
```
